32 devices in a mesh: blk: 4 (over x, core), shard: 8 (over z, y).
Axes of the slice: x: 2, y: 2, z: 4, core: 2. Of those that a mesh axis runs over, the one named last changes fastest.
Arguments:
- item_features: bfloat16 [32768, 1024], P('shard'), may hold values from -6 to 6
- tower_weight: bfloat16 [1024, 512], replicated, may hold values from -0.1875 to 0.1875
- gate_in: bfloat16 [64, 128], replicated, may hold values from -0.75 to 0.75
- gate_in_bias: bfloat16 [128], replicated, may hold values from -4 to 4
- gate_out: bfloat16 [128, 64], replicated, may hold values from -0.5 to 0.5
- gate_out_bias: bfloat16 [64], replicated, may hold values from -4 to 4
- user_table: bfloat16 [4096, 512], P(('blk', 'shard')), may hold values from -6 to 6
- user_ids: int32 [128], P(('blk', 'shard')), may hold values from 0 to 127
- positive_item: int32 [128, 16], P(('blk', 'shard')), may hold values from 0 to 2047
- listed_owner: int32 [128, 1], P(('blk', 'shard')), may hold values from 0 to 7; in each aligned block of 4 rows (0 to 3, 4 to 7, ...) at most 2 rows name the same one
- listed_slot: int32 [128], P(('blk', 'shard')), may hold values from 0 to 31
Outputs:
- tower_gradient: float32 [1024, 512], P('shard')
- user_gradient: float32 [4096, 512], P(('blk', 'shard'))
The draws below stay inside these ranges and needn't reach their ends.
Inputs may be any that keep to these rules, and one draw needn't show every extreme that they name: `listed_owner`: at most 2 of the 4 listings of one trainer name the same owner. `user_ids`: A row of the trainer's own 128 rows of user_table. `positive_item`: A position among the rows of the user's circle.
All inputs are finite; a program needn't handle non-finite values.
Results may differ from the reference program's by a relative error of at most 0.0055.
Values may be sent and summed in bfloat16 or wider, within the bound.
A program may use at most 128 MiB of HBM per device.

```python
import math
import jax
import jax.numpy as jnp
import numpy as np
from jax import lax

F = 1024
K = 8
H = 64
G = 128
BLK = 128
CAP = 2
POS = 16
OWN = 32
USERS = 4
UTAB = 128
LIST = 4
E = 512
P_SIZE = 64
GROUPS = 4
OWNERS = 8
TRAINERS = 32
CIRCLE = 2048


def plant(entries, stream_key, low, high):
    longest = entries.shape.index(max(entries.shape))
    spots = []
    for shift in (0, 1):
        where = [jax.random.randint(jax.random.fold_in(stream_key, axis), (), 0, length) for axis, length in enumerate(entries.shape)]
        where[longest] = (where[longest] + shift) % entries.shape[longest]
        spots.append(tuple(where))
    return entries.at[spots[0]].set(low).at[spots[1]].set(high)


def with_spikes(array, key, source, target, parts, factor):
    def block_of(axis_at):
        return (jnp.arange(array.shape[axis_at]) // (array.shape[axis_at] // parts)).reshape((-1,) + (1,) * (array.ndim - 1 - axis_at))

    near = jax.random.permutation(key, parts)[block_of(target)]
    far = (block_of(target) + parts // 2) % parts
    return jnp.where((block_of(source) == near) | (block_of(source) == far), factor * array, array)


def block_scale(stream_key, dims, cuts, low, high):
    loudness = 1.0
    for axis_at, parts in cuts:
        steps = jax.random.uniform(jax.random.fold_in(jax.random.fold_in(stream_key, 6), axis_at), (parts,), jnp.float32, low / len(cuts), high / len(cuts))
        loudness = loudness * jnp.repeat(jnp.exp(steps), dims[axis_at] // parts).reshape((-1,) + (1,) * (len(dims) - 1 - axis_at))
    return loudness


def assign_block(key, own, number, rows, amount, top, reach, slope):
    ranking = jax.random.permutation(key, amount)
    crowded, ordinary = shares(amount, rows * top, reach, slope, True), shares(amount, rows * top, reach, slope, False)
    places = jnp.arange(amount)

    def named(tallies, rotation):
        used = int((tallies > 0).sum())
        fixed = max(1, used // 4)
        shifted = fixed + (places - fixed + rotation * (used - fixed)) % max(1, amount - fixed)
        return jnp.zeros((amount,), jnp.int32).at[ranking[jnp.where(places < fixed, places, shifted)]].set(jnp.asarray(tallies, jnp.int32))

    tallies = jnp.where(number % 4 == 0, named(crowded, number // 4), named(ordinary, number - number // 4 - 1))
    mixed = jax.random.permutation(jax.random.fold_in(own, 3), amount)
    donor, sink = mixed[0:amount // 2 * 2:2], mixed[1:amount // 2 * 2:2]
    margin = jnp.minimum(tallies[donor] - 1, reach - tallies[sink]) // 2
    margin = jnp.where((donor == ranking[0]) | (sink == ranking[0]) | (tallies[sink] == 0), 0, jnp.maximum(margin, 0))
    shifted = jax.random.randint(jax.random.fold_in(own, 4), (amount // 2,), 0, 1 << 20) % (margin + 1)
    tallies = tallies.at[donor].add(-shifted).at[sink].add(shifted)
    labels = jnp.searchsorted(jnp.cumsum(tallies), jnp.arange(rows * top), side="right").astype(jnp.int32)
    grid = labels.reshape(top, rows).T
    grid = grid[jax.random.permutation(jax.random.fold_in(own, 1), rows)]
    rotation = jax.random.randint(jax.random.fold_in(own, 2), (rows, 1), 0, top)
    return jnp.take_along_axis(grid, (jnp.arange(top)[None, :] + rotation) % top, axis=1)


def shares(count, total, most, skew, full):
    portions = [(1 << 20) // math.isqrt(grade ** skew) + 1 for grade in range(1, count + 1)]
    largest = most if full else min(most, max(-(-total // count), total * portions[0] // sum(portions)))
    least = 1 if total - largest >= count - 1 else 0
    holding, surplus = [largest] + [least] * (count - 1), total - largest - least * (count - 1)
    while surplus > 0:
        candidates = [i for i in range(1, count) if holding[i] < largest] or [i for i in range(1, count) if holding[i] < most]
        pool, left = sum([portions[i] for i in candidates]), surplus
        for i in candidates:
            extra = min(most - holding[i], max(1, left * portions[i] // pool), surplus)
            holding[i] = holding[i] + extra
            surplus = surplus - extra
    return np.array(holding)


def noise(rng, shape, deviation, limit, split=(), kind=jnp.bfloat16):
    values = deviation * jax.random.normal(rng, shape, jnp.float32)
    if split:
        values = values * block_scale(rng, shape, split, -0.22, 0.18)
    return jnp.clip(values, -limit, limit).astype(kind)


def noise_with(rng, extent, width, limit, pieces, heavy, kind=jnp.bfloat16):
    entries = width * jax.random.normal(rng, extent, jnp.float32)
    if pieces:
        entries = entries * block_scale(rng, extent, pieces, -0.22, 0.18)
    return jnp.clip(with_spikes(entries, jax.random.fold_in(rng, 3), *heavy), -limit, limit).astype(kind)


def setup_inputs(seed: int = 0) -> dict:
    key_of = jax.random.split(jax.random.key(seed), 12)
    item_features = noise_with(key_of[0], (OWNERS * OWN * BLK, F), 1.0, 6.0, ((0, 8),), (0, 1, 8, 2.0))
    tower_weight = noise(key_of[1], (F, E), F ** -0.5, 0.1875)
    gate_in = noise(key_of[2], (P_SIZE, G), P_SIZE ** -0.5, 0.75)
    gate_in_bias = noise(key_of[3], (G,), 1.0, 4.0)
    gate_out = noise(key_of[4], (G, P_SIZE), G ** -0.5, 0.5)
    gate_out_bias = noise(key_of[5], (P_SIZE,), 1.0, 4.0)
    user_table = noise(key_of[6], (TRAINERS * UTAB, E), 1.0, 6.0, ((0, 32),))
    user_ids = plant(jax.random.randint(key_of[7], (TRAINERS * USERS,), 0, UTAB), jax.random.fold_in(key_of[7], 1), 0, UTAB - 1).astype(jnp.int32)
    positive_item = plant(jax.random.randint(key_of[8], (TRAINERS * USERS, POS), 0, CIRCLE), jax.random.fold_in(key_of[8], 1), 0, CIRCLE - 1).astype(jnp.int32)
    listed_owner_keys = jax.random.split(jax.random.fold_in(key_of[9], 1), (TRAINERS * LIST) // LIST)
    listed_owner_turns = jax.random.permutation(jax.random.fold_in(key_of[9], 3), (TRAINERS * LIST) // LIST)
    listed_owner = jax.vmap(lambda own, number: assign_block(jax.random.fold_in(key_of[9], 2), own, number, LIST, OWNERS, 1, CAP, 2))(listed_owner_keys, listed_owner_turns).reshape((TRAINERS * LIST, 1))
    listed_slot = plant(jax.random.randint(key_of[10], (TRAINERS * LIST,), 0, OWN), jax.random.fold_in(key_of[10], 1), 0, OWN - 1).astype(jnp.int32)
    return dict(item_features=item_features, tower_weight=tower_weight, gate_in=gate_in, gate_in_bias=gate_in_bias, gate_out=gate_out, gate_out_bias=gate_out_bias, user_table=user_table, user_ids=user_ids, positive_item=positive_item, listed_owner=listed_owner, listed_slot=listed_slot)


def pair_terms(user_rows, item_rows, targets, gate_in, gate_in_bias, gate_out, gate_out_bias):
    count_users = user_rows.shape[0]
    count_items = item_rows.shape[0]
    scaling = 1.0 / math.sqrt(H)
    user_parts = user_rows.astype(jnp.float32).reshape(count_users * K, H)
    item_parts = item_rows.astype(jnp.float32).reshape(count_items, K, H)
    logits = jnp.einsum('xh,ibh->xbi', user_parts, item_parts) * scaling
    logits = logits.reshape(count_users, K * K, count_items)
    gate_input = logits.astype(jnp.bfloat16)
    first_layer = gate_in.astype(jnp.float32)
    second_layer = gate_out.astype(jnp.float32)
    hidden_pre = jnp.einsum('pg,upi->ugi', first_layer, gate_input.astype(jnp.float32))
    hidden_pre = hidden_pre + gate_in_bias.astype(jnp.float32)[None, :, None]
    hidden = jax.nn.silu(hidden_pre).astype(jnp.bfloat16)
    gate_logit = jnp.einsum('gp,ugi->upi', second_layer, hidden.astype(jnp.float32))
    gate_logit = gate_logit + gate_out_bias.astype(jnp.float32)[None, :, None]
    exp_terms = jnp.exp(gate_logit)
    mixture = exp_terms / lax.optimization_barrier(jnp.sum(exp_terms, axis=1, keepdims=True))
    scores = lax.optimization_barrier(jnp.sum(mixture * logits, axis=1))
    score_grad = jax.nn.sigmoid(scores) - targets
    weighted = score_grad[:, None, :] * mixture
    logit_grad = (weighted * (logits - scores[:, None, :])).astype(jnp.bfloat16)
    gate_sig = jax.nn.sigmoid(hidden_pre)
    hidden_grad = jnp.einsum('gp,upi->ugi', second_layer, logit_grad.astype(jnp.float32))
    hidden_grad = (hidden_grad * gate_sig * (1.0 + hidden_pre * (1.0 - gate_sig))).astype(jnp.bfloat16)
    pair_grad = weighted + jnp.einsum('pg,ugi->upi', first_layer, hidden_grad.astype(jnp.float32))
    pair_grad = pair_grad.astype(jnp.bfloat16).astype(jnp.float32).reshape(count_users * K, K, count_items)
    user_delta = jnp.einsum('xbi,ibh->xh', pair_grad, item_parts).reshape(count_users, K * H) * scaling
    item_delta = jnp.einsum('xbi,xh->ibh', pair_grad, user_parts).reshape(count_items, K * H) * scaling
    return (user_delta, item_delta)

def reference(item_features, tower_weight, gate_in, gate_in_bias, gate_out, gate_out_bias, user_table, user_ids, positive_item, listed_owner, listed_slot):
    vectors = jnp.dot(item_features, tower_weight, preferred_element_type=jnp.float32).astype(jnp.bfloat16)
    vectors = vectors.reshape(OWNERS * OWN, BLK, E)
    block_ids = (listed_owner[:, 0] * OWN + listed_slot).astype(jnp.int32)
    listed = jnp.take(vectors, block_ids, axis=0).reshape(GROUPS, OWNERS, LIST * BLK, E)
    tables = user_table.reshape(TRAINERS, UTAB, E)
    row_ids = user_ids.reshape(TRAINERS, USERS).astype(jnp.int32)
    user_rows = jnp.take_along_axis(tables, row_ids[:, :, None], axis=1).reshape(GROUPS, OWNERS, USERS, E)
    targets = positive_item.reshape(GROUPS, OWNERS, USERS, POS)
    columns = jnp.arange(CIRCLE, dtype=jnp.int32)

    def column(column_index):
        col_users = lax.dynamic_index_in_dim(user_rows, column_index, 1, keepdims=False).reshape(GROUPS * USERS, E)
        col_items = lax.dynamic_index_in_dim(listed, column_index, 1, keepdims=False).reshape(CIRCLE, E)
        col_pos = lax.dynamic_index_in_dim(targets, column_index, 1, keepdims=False).reshape(GROUPS * USERS, POS)
        matches = jnp.any(col_pos[:, :, None] == columns[None, None, :], axis=1).astype(jnp.float32)
        return pair_terms(col_users, col_items, matches, gate_in, gate_in_bias, gate_out, gate_out_bias)
    user_delta, item_delta = lax.map(column, jnp.arange(OWNERS, dtype=jnp.int32))
    listing_grads = item_delta.astype(jnp.bfloat16).reshape(OWNERS, GROUPS, LIST, BLK, E)
    listing_grads = jnp.transpose(listing_grads, (1, 0, 2, 3, 4)).reshape(TRAINERS * LIST, BLK, E)
    per_block = jax.ops.segment_sum(listing_grads.astype(jnp.float32), block_ids, num_segments=OWNERS * OWN)
    per_block = per_block.reshape(OWNERS * OWN * BLK, E)
    tower_gradient = lax.dot_general(item_features.astype(jnp.float32), per_block, (((0,), (0,)), ((), ())), precision=lax.Precision.HIGHEST)
    user_deltas = jnp.transpose(user_delta.reshape(OWNERS, GROUPS, USERS, E), (1, 0, 2, 3)).reshape(TRAINERS, USERS, E)
    row_hot = (row_ids[:, :, None] == jnp.arange(UTAB, dtype=jnp.int32)[None, None, :]).astype(jnp.float32)
    user_gradient = jnp.einsum('tkr,tke->tre', row_hot, user_deltas, precision=lax.Precision.HIGHEST)
    return (tower_gradient, user_gradient.reshape(TRAINERS * UTAB, E))
```

```python
import functools
import math

import jax
import jax.numpy as jnp
from jax import lax
from jax.experimental import pallas as pl
from jax.experimental.pallas import tpu as pltpu
from jax.sharding import PartitionSpec as P

K = 8
H = 64
BLK = 128
CAP = 2
LANES = 128
CORES = 2
UNITS = 2
CHUNK = 8
TOWER_PIECES = 2
ACC_PIECES = 4
RING = 4

NN = (((1,), (0,)), ((), ()))
NT = (((1,), (1,)), ((), ()))
MESH = pl.DeviceIdType.MESH


def dot(left, right, dims=NN):
    return lax.dot_general(left, right, dims, preferred_element_type=jnp.float32)


def gather_kernel(
    groups,
    owners,
    ids_ref,
    pos_ref,
    owner_ref,
    slot_ref,
    table_ref,
    tower_hbm,
    users_out,
    lines_out,
    tower_t_ref,
    users,
    lines,
    tower_s,
    tower_sem,
    send1,
    recv1,
    send2,
    recv2,
):
    g = lax.axis_index("blk")
    s = lax.axis_index("shard")
    chips = groups // CORES
    core = lax.rem(g, CORES)
    chip = g // CORES
    sister = chip * CORES + (CORES - 1) - core
    partners = [(c, d) for c in range(chips) for d in range(owners) if c or d]

    def device(c, d):
        return (lax.rem(chip + c, chips) * CORES + core, lax.rem(s + d, owners))

    barrier = pltpu.get_barrier_semaphore()
    for c, d in partners:
        pl.semaphore_signal(barrier, inc=1, device_id=device(c, d), device_id_type=MESH)
    pl.semaphore_signal(barrier, inc=1, device_id=(sister, s), device_id_type=MESH)
    fetch = pltpu.make_async_copy(tower_hbm, tower_s, tower_sem)
    fetch.start()

    count, picks = pos_ref.shape
    listings = slot_ref.shape[0]
    half = count // 2
    table, embed = table_ref.shape
    rows = half * K
    row = lax.broadcasted_iota(jnp.int32, (rows, table), 0)
    column = lax.broadcasted_iota(jnp.int32, (rows, table), 1)
    block = lax.broadcasted_iota(jnp.int32, (rows, embed), 1) // H
    mine = block == lax.broadcasted_iota(jnp.int32, (rows, embed), 0) % K
    parts = []
    for part in range(2):
        wanted = jnp.zeros((rows, table), jnp.int32)
        for k in range(half):
            wanted = jnp.where(row // K == k, ids_ref[part * half + k], wanted)
        picked = dot(jnp.where(column == wanted, 1.0, 0.0).astype(jnp.bfloat16), table_ref[...])
        picked = jnp.where(mine, picked * (1.0 / math.sqrt(H)), 0.0)
        total = picked[:, :LANES]
        for first in range(LANES, embed, LANES):
            total = total + picked[:, first : first + LANES]
        parts.append(total + pltpu.roll(total, H, 1))
    lane = lax.broadcasted_iota(jnp.int32, (rows, LANES), 1)
    users[core, chip, s] = jnp.where(lane < H, parts[0], parts[1]).astype(jnp.bfloat16)
    lane = lax.broadcasted_iota(jnp.int32, (1, LANES), 1)
    line = jnp.zeros((1, LANES), jnp.int32)
    for k in range(count):
        for p in range(picks):
            line = jnp.where(lane == k * picks + p, pos_ref[k, p], line)
    for j in range(listings):
        line = jnp.where(lane == count * picks + j, owner_ref[0, j], line)
        line = jnp.where(lane == count * picks + listings + j, slot_ref[j], line)
    lines[core, chip, s] = line

    pl.semaphore_wait(barrier, len(partners) + 1)
    copies = []
    for n, (c, d) in enumerate(partners):
        for m, ref in enumerate((users, lines)):
            copy = pltpu.make_async_remote_copy(
                src_ref=ref.at[core, chip, s], dst_ref=ref.at[core, chip, s],
                send_sem=send1.at[m, n], recv_sem=recv1.at[m, n],
                device_id=device(c, d), device_id_type=MESH,
            )
            copy.start()
            copies.append(copy)
    fetch.wait()
    tower_t_ref[...] = tower_s[...].T
    for copy in copies:
        copy.wait()
    copies = []
    for m, ref in enumerate((users, lines)):
        copy = pltpu.make_async_remote_copy(
            src_ref=ref.at[core], dst_ref=ref.at[core],
            send_sem=send2.at[m], recv_sem=recv2.at[m],
            device_id=(sister, s), device_id_type=MESH,
        )
        copy.start()
        copies.append(copy)
    for copy in copies:
        copy.wait()
    users_out[...] = users[...]
    lines_out[...] = lines[...]


def pair_kernel(
    groups,
    owners,
    users,
    picks,
    listings,
    lists_ref,
    feat_hbm,
    tower_ref,
    users_ref,
    lines_ref,
    gin_in,
    gin_b_in,
    gout_in,
    gout_b_in,
    out_ref,
    acc,
    uacc,
    logit_s,
    feat_s,
    vec_s,
    grad_s,
    feat_sem,
    slots,
    columns,
    bases,
    gin_ref,
    gin_t_ref,
    gout_ref,
    gout_t_ref,
):
    g = lax.axis_index("blk")
    s = lax.axis_index("shard")
    chips = groups // CORES
    column_users = groups * users
    half = users // 2
    pairs = K * K
    hidden = gin_in.shape[1]
    embed, features = tower_ref.shape
    first_owner = users * picks

    def scan(row, carry):
        n, turn = carry
        place = row // owners
        group = lax.rem(place, chips) * CORES + place // chips
        for j in range(listings):
            mine = lists_ref[row, 0, first_owner + j] == s
            slots[n] = lists_ref[row, 0, first_owner + listings + j]
            columns[n] = lax.rem(row, owners)
            bases[n] = (group * listings + j) * BLK
            n = n + jnp.where(jnp.logical_and(mine, turn == g), 1, 0)
            turn = jnp.where(mine, jnp.where(turn == groups - 1, 0, turn + 1), turn)
        return n, turn

    zero = jnp.int32(0)
    count, _ = lax.fori_loop(0, groups * owners, scan, (zero, zero))
    steps = (count + UNITS - 1) // UNITS

    def fetch(step):
        slot = lax.rem(step, RING)
        copies = []
        for j in range(UNITS):
            n = jnp.minimum(step * UNITS + j, count - 1)
            copies.append(
                pltpu.make_async_copy(
                    feat_hbm.at[pl.ds(pl.multiple_of(slots[n] * BLK, BLK), BLK)],
                    feat_s.at[slot, pl.ds(j * BLK, BLK)],
                    feat_sem.at[slot, j],
                )
            )
        return copies

    @pl.when(count > 0)
    def _():
        for copy in fetch(zero):
            copy.start()

    @pl.when(steps > 1)
    def _():
        for copy in fetch(zero + 1):
            copy.start()

    acc[...] = jnp.zeros_like(acc)
    uacc[...] = jnp.zeros_like(uacc)
    grad_s[...] = jnp.zeros_like(grad_s)
    to = lax.broadcasted_iota(jnp.int32, (pairs, pairs), 0)
    of = lax.broadcasted_iota(jnp.int32, (pairs, pairs), 1)
    turn = jnp.where(of == (to % K) * K + to // K, 1.0, 0.0).astype(jnp.bfloat16)

    def beside(row, scale):
        column = jnp.broadcast_to(row.astype(jnp.float32), (LANES, row.shape[1])).T[:, :16]
        lane = lax.broadcasted_iota(jnp.int32, column.shape, 1)
        return jnp.where(lane == 0, column * scale, 0.0).astype(jnp.bfloat16)

    gin = dot(turn, gin_in[...])
    gin_ref[...] = gin.astype(jnp.bfloat16)
    gin_t_ref[:, :pairs] = (0.5 * gin.T).astype(jnp.bfloat16)
    gin_t_ref[:, pairs:] = beside(gin_b_in[...], 0.5)
    gout_t = dot(turn, gout_in[...])
    gout_ref[...] = (0.5 * gout_t.T).astype(jnp.bfloat16)
    gout_t_ref[:, :hidden] = gout_t.astype(jnp.bfloat16)
    gout_t_ref[:, hidden:] = dot(turn, beside(gout_b_in[...], 1.0)).astype(jnp.bfloat16)
    ones = jnp.ones((16, CHUNK * BLK), jnp.bfloat16)
    order = [
        (r, part * half + k) for part in range(2) for r in range(groups) for k in range(half)
    ]

    def tower_piece(m, step, slot):
        rows = pl.ds(m * (embed // TOWER_PIECES), embed // TOWER_PIECES)
        vectors = dot(tower_ref[rows, :], feat_s[lax.rem(step, RING)], NT)
        vec_s[slot, rows] = vectors.astype(jnp.bfloat16)

    def acc_piece(c, step, slot):
        cut = pl.ds(c * (features // ACC_PIECES), features // ACC_PIECES)
        acc[:, cut] += dot(grad_s[slot], feat_s[lax.rem(step, RING), :, cut])

    def prepare(step, unit):
        n = jnp.minimum(step * UNITS + unit, count - 1)
        slot = lax.rem(step, 2)
        vec = vec_s[slot, :, unit * BLK : (unit + 1) * BLK]
        vec_cat = jnp.concatenate([vec[b * H : (b + 1) * H] for b in range(K)], axis=1)
        column = columns[n]
        near = [(r % CORES, r // CORES, column) for r in range(groups)]
        packed = jnp.concatenate([users_ref[at] for at in near], axis=0)
        vectors = jnp.concatenate([packed[:, :H], packed[:, H:]], axis=0)
        logit_s[unit] = dot(vectors, vec_cat)
        lines = jnp.concatenate([lines_ref[at] for at in near], axis=0)
        place = bases[n] + lax.broadcasted_iota(jnp.int32, (groups, BLK), 1)
        targets = []
        for k in range(users):
            hit = lines[:, k * picks : k * picks + 1] == place
            for p in range(k * picks + 1, (k + 1) * picks):
                hit = jnp.logical_or(hit, lines[:, p : p + 1] == place)
            targets.append(jnp.where(hit, 1.0, 0.0))
        return dict(
            unit=unit,
            slot=slot,
            column=column,
            valid=jnp.where(step * UNITS + unit < count, 1.0, 0.0),
            vec_cat=vec_cat,
            vectors=vectors,
            targets=targets,
            rows=[],
        )

    def chunk(state, first):
        unit = state["unit"]
        picked = range(first, first + CHUNK)
        logits = jnp.concatenate(
            [
                jnp.concatenate(
                    [
                        logit_s[unit, u * K : (u + 1) * K, b * BLK : (b + 1) * BLK]
                        for b in range(K)
                    ],
                    axis=0,
                )
                for u in picked
            ],
            axis=1,
        )
        wanted = jnp.concatenate(
            [state["targets"][order[u][1]][order[u][0] : order[u][0] + 1] for u in picked], axis=1
        )
        half_pre = dot(
            gin_t_ref[...], jnp.concatenate([logits.astype(jnp.bfloat16), ones], axis=0)
        )
        yield
        t = jnp.tanh(half_pre)
        up = 1.0 + t
        silu = half_pre * up
        slope = up + silu * (1.0 - t)
        gate = dot(gout_t_ref[...], jnp.concatenate([silu.astype(jnp.bfloat16), ones], axis=0))
        yield
        terms = jnp.exp(gate)
        mixture = terms * (1.0 / jnp.sum(terms, axis=0, keepdims=True))
        scores = jnp.sum(mixture * logits, axis=0, keepdims=True)
        score_grad = (0.5 + 0.5 * jnp.tanh(0.5 * scores) - wanted) * state["valid"]
        weighted = score_grad * mixture
        logit_grad = (weighted * (logits - scores)).astype(jnp.bfloat16)
        back = dot(gout_ref[...], logit_grad)
        yield
        hidden_grad = (back * slope).astype(jnp.bfloat16)
        more = dot(gin_ref[...], hidden_grad)
        yield
        pair = weighted + more
        for n in range(CHUNK):
            state["rows"].append(
                jnp.concatenate(
                    [
                        pair[b * K : (b + 1) * K, n * BLK : (n + 1) * BLK]
                        for b in range(K)
                    ],
                    axis=1,
                )
            )
        if len(state["rows"]) == column_users:
            pair_all = jnp.concatenate(state["rows"], axis=0).astype(jnp.bfloat16)
            uacc[state["column"]] += dot(pair_all, state["vec_cat"], NT)
            vectors_t = state["vectors"].astype(jnp.float32).T.astype(jnp.bfloat16)
            grad = dot(vectors_t, pair_all).astype(jnp.bfloat16)
            grad_s[state["slot"], :, unit * BLK : (unit + 1) * BLK] = jnp.concatenate(
                [grad[:, b * BLK : (b + 1) * BLK] for b in range(K)], axis=0
            )
        yield

    stages = 5

    def step_body(step, carry):
        @pl.when(step + 2 < steps)
        def _():
            for copy in fetch(step + 2):
                copy.start()

        @pl.when(step + 1 < steps)
        def _():
            for copy in fetch(step + 1):
                copy.wait()

        before = jnp.maximum(step - 1, 0)
        after = jnp.minimum(step + 1, steps - 1)
        other = lax.rem(step + 1, 2)
        extras = [functools.partial(tower_piece, m, after, other) for m in range(TOWER_PIECES)]
        extras += [functools.partial(acc_piece, c, before, other) for c in range(ACC_PIECES)]
        states = [prepare(step, unit) for unit in range(UNITS)]
        chunks = [
            chunk(state, first) for state in states for first in range(0, column_users, CHUNK)
        ]
        waves = len(chunks) + stages - 1
        done = 0
        for wave in range(waves):
            for n, work in enumerate(chunks):
                if 0 <= wave - n < stages:
                    next(work)
            while done < len(extras) * (wave + 1) // waves:
                extras[done]()
                done += 1
        return carry

    @pl.when(count > 0)
    def _():
        for copy in fetch(zero):
            copy.wait()
        for m in range(TOWER_PIECES):
            tower_piece(m, zero, 0)
        lax.fori_loop(0, steps, step_body, 0)
        for c in range(ACC_PIECES):
            acc_piece(c, steps - 1, lax.rem(steps - 1, 2))

    width = features // owners
    height = embed // groups
    share = half * K
    if width < LANES:
        out_ref[...] = jnp.zeros_like(out_ref)
    for r in range(groups):
        for d in range(owners):
            out_ref[d, r % CORES, r // CORES, 0:height, 0:width] = acc[
                r * height : (r + 1) * height, d * width : (d + 1) * width
            ].astype(jnp.bfloat16)
            parts = [
                uacc[d, (part * groups + r) * share : (part * groups + r + 1) * share]
                for part in range(2)
            ]
            out_ref[d, r % CORES, r // CORES, height : height + share, :] = (
                jnp.concatenate(parts, axis=1) * (1.0 / math.sqrt(H))
            ).astype(jnp.bfloat16)


def sum_kernel(
    groups,
    owners,
    in_ref,
    part_out,
    user_out,
    recv0,
    both,
    recv1,
    stage,
    recv2,
    part,
    final,
    send0,
    rsem0,
    send1,
    rsem1,
    send2,
    rsem2,
    send3,
    rsem3,
):
    g = lax.axis_index("blk")
    s = lax.axis_index("shard")
    height = part.shape[0]
    chips = groups // CORES
    core = lax.rem(g, CORES)
    chip = g // CORES
    sister = chip * CORES + (CORES - 1) - core

    def peer(d):
        if owners & (owners - 1):
            return lax.rem(s + d, owners)
        to = s
        bit = 1
        while bit < owners:
            if d & bit:
                to = to + bit * (1 - 2 * lax.rem(s // bit, 2))
            bit *= 2
        return to

    barrier = pltpu.get_barrier_semaphore()
    for d in range(1, groups):
        pl.semaphore_signal(
            barrier, inc=1, device_id=(lax.rem(g + d, groups), s), device_id_type=MESH
        )
    for d in range(1, owners):
        pl.semaphore_signal(barrier, inc=1, device_id=(g, peer(d)), device_id_type=MESH)
    pl.semaphore_wait(barrier, groups + owners - 2)

    order = list(range(owners - 1, -1, -1))
    first = []
    for n, d in enumerate(order):
        copy = pltpu.make_async_remote_copy(
            src_ref=in_ref.at[peer(d), CORES - 1 - core], dst_ref=recv0.at[n],
            send_sem=send0.at[n], recv_sem=rsem0.at[n],
            device_id=(sister, s), device_id_type=MESH,
        )
        copy.start()
        first.append(copy)
    second = []
    for n, d in enumerate(order):
        first[n].wait()
        second.append([])
        for c in range(1, chips):
            to = lax.rem(chip + c, chips)
            both[n, c - 1] = (
                in_ref[peer(d), core, to].astype(jnp.float32) + recv0[n, to].astype(jnp.float32)
            ).astype(jnp.bfloat16)
            copy = pltpu.make_async_remote_copy(
                src_ref=both.at[n, c - 1], dst_ref=recv1.at[n, c - 1],
                send_sem=send1.at[n, c - 1], recv_sem=rsem1.at[n, c - 1],
                device_id=(to * CORES + core, s), device_id_type=MESH,
            )
            copy.start()
            second[n].append(copy)
    third = []
    total = None
    for n, d in enumerate(order):
        for copy in second[n]:
            copy.wait()
        total = in_ref[peer(d), core, chip].astype(jnp.float32) + recv0[n, chip].astype(jnp.float32)
        for c in range(1, chips):
            total = total + recv1[n, c - 1].astype(jnp.float32)
        if d:
            stage[n] = total.astype(jnp.bfloat16)
            copy = pltpu.make_async_remote_copy(
                src_ref=stage.at[n], dst_ref=recv2.at[n],
                send_sem=send2.at[n], recv_sem=rsem2.at[n],
                device_id=(g, peer(d)), device_id_type=MESH,
            )
            copy.start()
            third.append(copy)
    for n, copy in enumerate(third):
        copy.wait()
        total = total + recv2[n].astype(jnp.float32)
    user_out[...] = total[height:]
    part[...] = total[:height].astype(jnp.bfloat16)

    copies = []
    for d in range(1, groups):
        copy = pltpu.make_async_remote_copy(
            src_ref=part, dst_ref=final.at[g],
            send_sem=send3.at[d - 1], recv_sem=rsem3.at[d - 1],
            device_id=(lax.rem(g + d, groups), s), device_id_type=MESH,
        )
        copy.start()
        copies.append(copy)
    final[g] = part[...]
    for copy in copies:
        copy.wait()
    part_out[...] = final[...]


def finish_kernel(users, ids_ref, part_ref, user_ref, tower_out, user_out):
    groups, height, _ = part_ref.shape
    width = tower_out.shape[0]
    for r in range(groups):
        tower_out[:, r * height : (r + 1) * height] = part_ref[r].astype(jnp.float32).T[:width]
    half = users // 2
    straight = user_ref[...]
    turned = pltpu.roll(straight, H, 1)
    table, embed = user_out.shape
    row = lax.broadcasted_iota(jnp.int32, (table, LANES), 0)
    low = lax.broadcasted_iota(jnp.int32, (1, LANES), 1) < H
    for first in range(0, embed, LANES):
        total = jnp.zeros((table, LANES), jnp.float32)
        for k in range(users):
            at = (k % half) * K + first // H
            left, right = (straight, turned) if k < half else (turned, straight)
            line = jnp.where(low, left[at : at + 1], right[at + 1 : at + 2])
            total = total + jnp.where(row == ids_ref[k], line, 0.0)
        user_out[:, first : first + LANES] = total


def shards(
    item_features,
    tower_weight,
    gate_in,
    gate_in_bias,
    gate_out,
    gate_out_bias,
    user_table,
    user_ids,
    positive_item,
    listed_owner,
    listed_slot,
):
    groups = lax.axis_size("blk")
    owners = lax.axis_size("shard")
    chips = groups // CORES
    trainers = groups * owners
    listings = listed_slot.shape[0]
    users, picks = positive_item.shape
    table = user_table.shape[0]
    features = item_features.shape[1]
    embed = tower_weight.shape[1]
    hidden = gate_in.shape[1]
    pairs = K * K
    rows = groups * users * K
    share = users // 2 * K
    bf16, f32, i32 = jnp.bfloat16, jnp.float32, jnp.int32
    vmem = pl.BlockSpec(memory_space=pltpu.VMEM)
    smem = pl.BlockSpec(memory_space=pltpu.SMEM)
    hbm = pl.BlockSpec(memory_space=pl.ANY)
    dma = pltpu.SemaphoreType.DMA
    partners = chips * owners - 1

    all_users, all_lines, tower_t = pl.pallas_call(
        functools.partial(gather_kernel, groups, owners),
        out_shape=(
            jax.ShapeDtypeStruct((CORES, chips, owners, share, LANES), bf16),
            jax.ShapeDtypeStruct((CORES, chips, owners, 1, LANES), i32),
            jax.ShapeDtypeStruct((embed, features), bf16),
        ),
        in_specs=[smem, smem, smem, smem, vmem, hbm],
        out_specs=(vmem, vmem, vmem),
        scratch_shapes=[
            pltpu.VMEM((CORES, chips, owners, share, LANES), bf16),
            pltpu.VMEM((CORES, chips, owners, 1, LANES), i32),
            pltpu.VMEM((features, embed), bf16),
            dma,
            dma((2, partners)),
            dma((2, partners)),
            dma((2,)),
            dma((2,)),
        ],
        compiler_params=pltpu.CompilerParams(collective_id=1, has_side_effects=True),
        name="gather_users",
    )(user_ids, positive_item, listed_owner.T, listed_slot, user_table, tower_weight)

    most = -(-trainers * min(CAP, listings) // groups)
    height = embed // groups
    width = features // owners
    terms = pl.pallas_call(
        functools.partial(pair_kernel, groups, owners, users, picks, listings),
        out_shape=jax.ShapeDtypeStruct((owners, CORES, chips, height + share, LANES), bf16),
        in_specs=[smem, hbm] + [vmem] * 7,
        out_specs=vmem,
        scratch_shapes=[
            pltpu.VMEM((embed, features), f32),
            pltpu.VMEM((owners, rows, H), f32),
            pltpu.VMEM((UNITS, rows, K * BLK), f32),
            pltpu.VMEM((RING, UNITS * BLK, features), bf16),
            pltpu.VMEM((2, embed, UNITS * BLK), bf16),
            pltpu.VMEM((2, embed, UNITS * BLK), bf16),
            dma((RING, UNITS)),
            pltpu.SMEM((most + 1,), i32),
            pltpu.SMEM((most + 1,), i32),
            pltpu.SMEM((most + 1,), i32),
            pltpu.VMEM((pairs, hidden), bf16),
            pltpu.VMEM((hidden, pairs + 16), bf16),
            pltpu.VMEM((hidden, pairs), bf16),
            pltpu.VMEM((pairs, hidden + 16), bf16),
        ],
        compiler_params=pltpu.CompilerParams(vmem_limit_bytes=56 << 20),
        name="pair_terms",
    )(
        all_lines.reshape(trainers, 1, LANES),
        item_features,
        tower_t,
        all_users,
        all_lines,
        gate_in,
        gate_in_bias[None, :],
        gate_out.T,
        gate_out_bias[None, :],
    )

    block = (height + share, LANES)
    part, user_terms = pl.pallas_call(
        functools.partial(sum_kernel, groups, owners),
        out_shape=(
            jax.ShapeDtypeStruct((groups, height, LANES), bf16),
            jax.ShapeDtypeStruct((share, LANES), f32),
        ),
        in_specs=[vmem],
        out_specs=(vmem, vmem),
        scratch_shapes=[
            pltpu.VMEM((owners, chips) + block, bf16),
            pltpu.VMEM((owners, chips - 1) + block, bf16),
            pltpu.VMEM((owners, chips - 1) + block, bf16),
            pltpu.VMEM((owners - 1,) + block, bf16),
            pltpu.VMEM((owners - 1,) + block, bf16),
            pltpu.VMEM((height, LANES), bf16),
            pltpu.VMEM((groups, height, LANES), bf16),
            dma((owners,)),
            dma((owners,)),
            dma((owners, chips - 1)),
            dma((owners, chips - 1)),
            dma((owners - 1,)),
            dma((owners - 1,)),
            dma((groups - 1,)),
            dma((groups - 1,)),
        ],
        compiler_params=pltpu.CompilerParams(collective_id=0, has_side_effects=True),
        name="sum_terms",
    )(terms)

    return pl.pallas_call(
        functools.partial(finish_kernel, users),
        out_shape=(
            jax.ShapeDtypeStruct((width, embed), f32),
            jax.ShapeDtypeStruct((table, embed), f32),
        ),
        in_specs=[smem, vmem, vmem],
        out_specs=(vmem, vmem),
        name="finish",
    )(user_ids, part, user_terms)


def solution(mesh):
    return jax.shard_map(
        shards,
        mesh=mesh,
        in_specs=(
            P("shard", None),
            P(),
            P(),
            P(),
            P(),
            P(),
            P(("blk", "shard"), None),
            P(("blk", "shard")),
            P(("blk", "shard"), None),
            P(("blk", "shard"), None),
            P(("blk", "shard")),
        ),
        out_specs=(P("shard", None), P(("blk", "shard"), None)),
        check_vma=False,
    )
```

```python
import functools
import math

import jax
import jax.numpy as jnp
from jax import lax
from jax.experimental import pallas as pl
from jax.experimental.pallas import tpu as pltpu
from jax.sharding import PartitionSpec as P

K = 8
H = 64
BLK = 128
CAP = 2
LANES = 128
CORES = 2
UNITS = 2
CHUNK = 8
TOWER_PIECES = 2
ACC_PIECES = 4
RING = 4
SCAN_ROWS = 4

NN = (((1,), (0,)), ((), ()))
NT = (((1,), (1,)), ((), ()))
MESH = pl.DeviceIdType.MESH


def dot(left, right, dims=NN):
    return lax.dot_general(left, right, dims, preferred_element_type=jnp.float32)


def gather_kernel(
    groups,
    owners,
    ids_hbm,
    pos_hbm,
    owner_hbm,
    slot_hbm,
    table_hbm,
    gin_hbm,
    gin_b_hbm,
    gout_hbm,
    gout_b_hbm,
    tower_hbm,
    users_out,
    lines_out,
    gin_ref,
    gin_t_ref,
    gout_ref,
    gout_t_ref,
    tower_t_ref,
    users,
    lines,
    ids_ref,
    pos_ref,
    owner_ref,
    slot_ref,
    table_ref,
    gin_in,
    gin_b_in,
    gout_in,
    gout_b_in,
    tower_s,
    load_sem,
    send1,
    recv1,
    send2,
    recv2,
):
    g = lax.axis_index("blk")
    s = lax.axis_index("shard")
    chips = groups // CORES
    core = lax.rem(g, CORES)
    chip = g // CORES
    sister = chip * CORES + (CORES - 1) - core
    partners = [(c, d) for c in range(chips) for d in range(owners) if c or d]

    def device(c, d):
        return (lax.rem(chip + c, chips) * CORES + core, lax.rem(s + d, owners))

    barrier = pltpu.get_barrier_semaphore()
    for c, d in partners:
        pl.semaphore_signal(barrier, inc=1, device_id=device(c, d), device_id_type=MESH)
    pl.semaphore_signal(barrier, inc=1, device_id=(sister, s), device_id_type=MESH)
    loads = [
        pltpu.make_async_copy(source, to, load_sem.at[n])
        for n, (source, to) in enumerate(
            (
                (ids_hbm, ids_ref),
                (pos_hbm, pos_ref),
                (owner_hbm, owner_ref),
                (slot_hbm, slot_ref),
                (table_hbm, table_ref),
                (gin_hbm, gin_in),
                (gin_b_hbm, gin_b_in),
                (gout_hbm, gout_in),
                (gout_b_hbm, gout_b_in),
                (tower_hbm, tower_s),
            )
        )
    ]
    for copy in loads:
        copy.start()
    for copy in loads[:5]:
        copy.wait()

    count, picks = pos_ref.shape
    listings = slot_ref.shape[0]
    half = count // 2
    table, embed = table_ref.shape
    rows = half * K
    row = lax.broadcasted_iota(jnp.int32, (rows, table), 0)
    column = lax.broadcasted_iota(jnp.int32, (rows, table), 1)
    block = lax.broadcasted_iota(jnp.int32, (rows, embed), 1) // H
    mine = block == lax.broadcasted_iota(jnp.int32, (rows, embed), 0) % K
    parts = []
    for part in range(2):
        wanted = jnp.zeros((rows, table), jnp.int32)
        for k in range(half):
            wanted = jnp.where(row // K == k, ids_ref[part * half + k], wanted)
        picked = dot(jnp.where(column == wanted, 1.0, 0.0).astype(jnp.bfloat16), table_ref[...])
        picked = jnp.where(mine, picked * (1.0 / math.sqrt(H)), 0.0)
        total = picked[:, :LANES]
        for first in range(LANES, embed, LANES):
            total = total + picked[:, first : first + LANES]
        parts.append(total + pltpu.roll(total, H, 1))
    lane = lax.broadcasted_iota(jnp.int32, (rows, LANES), 1)
    users[core, chip, s] = jnp.where(lane < H, parts[0], parts[1]).astype(jnp.bfloat16)
    lane = lax.broadcasted_iota(jnp.int32, (1, LANES), 1)
    line = jnp.zeros((1, LANES), jnp.int32)
    for k in range(count):
        for p in range(picks):
            line = jnp.where(lane == k * picks + p, pos_ref[k, p], line)
    for j in range(listings):
        line = jnp.where(lane == count * picks + j, owner_ref[0, j], line)
        line = jnp.where(lane == count * picks + listings + j, slot_ref[j], line)
    lines[core, chip, s] = line

    pl.semaphore_wait(barrier, len(partners) + 1)
    copies = []
    for n, (c, d) in enumerate(partners):
        for m, ref in enumerate((users, lines)):
            copy = pltpu.make_async_remote_copy(
                src_ref=ref.at[core, chip, s], dst_ref=ref.at[core, chip, s],
                send_sem=send1.at[m, n], recv_sem=recv1.at[m, n],
                device_id=device(c, d), device_id_type=MESH,
            )
            copy.start()
            copies.append(copy)
    for copy in loads[5:]:
        copy.wait()
    tower_t_ref[...] = tower_s[...].T
    pairs, hidden = gin_in.shape
    to = lax.broadcasted_iota(jnp.int32, (pairs, pairs), 0)
    of = lax.broadcasted_iota(jnp.int32, (pairs, pairs), 1)
    turn = jnp.where(of == (to % K) * K + to // K, 1.0, 0.0).astype(jnp.bfloat16)

    def beside(row, scale):
        column = jnp.broadcast_to(row.astype(jnp.float32), (LANES, row.shape[1])).T[:, :16]
        lane = lax.broadcasted_iota(jnp.int32, column.shape, 1)
        return jnp.where(lane == 0, column * scale, 0.0).astype(jnp.bfloat16)

    gin = dot(turn, gin_in[...])
    gin_ref[...] = gin.astype(jnp.bfloat16)
    gin_t_ref[:, :pairs] = (0.5 * gin.T).astype(jnp.bfloat16)
    gin_t_ref[:, pairs:] = beside(gin_b_in[...], 0.5)
    gout_t = dot(turn, gout_in[...])
    gout_ref[...] = (0.5 * gout_t.T).astype(jnp.bfloat16)
    gout_t_ref[:, :hidden] = gout_t.astype(jnp.bfloat16)
    gout_t_ref[:, hidden:] = dot(turn, beside(gout_b_in[...], 1.0)).astype(jnp.bfloat16)
    for copy in copies:
        copy.wait()
    copies = []
    for m, ref in enumerate((users, lines)):
        copy = pltpu.make_async_remote_copy(
            src_ref=ref.at[core], dst_ref=ref.at[core],
            send_sem=send2.at[m], recv_sem=recv2.at[m],
            device_id=(sister, s), device_id_type=MESH,
        )
        copy.start()
        copies.append(copy)
    for copy in copies:
        copy.wait()
    users_out[...] = users[...]
    lines_out[...] = lines[...]


def pair_kernel(
    groups,
    owners,
    users,
    picks,
    listings,
    lists_ref,
    feat_hbm,
    users_hbm,
    lines_hbm,
    gin_hbm,
    gin_t_hbm,
    gout_hbm,
    gout_t_hbm,
    tower_hbm,
    out_hbm,
    users_ref,
    lines_ref,
    gin_ref,
    gin_t_ref,
    gout_ref,
    gout_t_ref,
    tower_ref,
    out_ref,
    acc,
    uacc,
    logit_s,
    feat_s,
    vec_s,
    grad_s,
    feat_sem,
    load_sem,
    out_sem,
    entries,
):
    g = lax.axis_index("blk")
    s = lax.axis_index("shard")
    chips = groups // CORES
    column_users = groups * users
    half = users // 2
    embed, features = tower_ref.shape
    first_owner = users * picks

    loads = [
        pltpu.make_async_copy(source, to, load_sem.at[n])
        for n, (source, to) in enumerate(
            (
                (tower_hbm, tower_ref),
                (users_hbm, users_ref),
                (lines_hbm, lines_ref),
                (gin_hbm, gin_ref),
                (gin_t_hbm, gin_t_ref),
                (gout_hbm, gout_ref),
                (gout_t_hbm, gout_t_ref),
            )
        )
    ]
    for copy in loads:
        copy.start()

    def scan(turn, n):
        for row in range(SCAN_ROWS):
            for j in range(listings):
                entries[n] = (turn * SCAN_ROWS + row) * listings + j
                mine = lists_ref[turn * SCAN_ROWS + row, 0, first_owner + j] == s
                n = n + mine.astype(jnp.int32)
        return n

    zero = jnp.int32(0)
    listed = lax.fori_loop(0, groups * owners // SCAN_ROWS, scan, zero)
    count = (listed + groups - 1 - g) // groups
    steps = (count + UNITS - 1) // UNITS

    def find(step, unit):
        n = jnp.minimum(step * UNITS + unit, count - 1)
        entry = entries[n * groups + g]
        row = entry // listings
        j = entry - row * listings
        place = row // owners
        group = lax.rem(place, chips) * CORES + place // chips
        slot = lists_ref[row, 0, first_owner + listings + j]
        return slot, lax.rem(row, owners), (group * listings + j) * BLK

    def fetch(step):
        copies = []
        for j in range(UNITS):
            block, _, _ = find(step, j)
            copies.append(
                pltpu.make_async_copy(
                    feat_hbm.at[pl.ds(pl.multiple_of(block * BLK, BLK), BLK)],
                    feat_s.at[lax.rem(step, RING), pl.ds(j * BLK, BLK)],
                    feat_sem.at[lax.rem(step, RING), j],
                )
            )
        return copies

    @pl.when(count > 0)
    def _():
        for copy in fetch(zero):
            copy.start()

    @pl.when(steps > 1)
    def _():
        for copy in fetch(zero + 1):
            copy.start()

    acc[...] = jnp.zeros_like(acc)
    uacc[...] = jnp.zeros_like(uacc)
    grad_s[...] = jnp.zeros_like(grad_s)
    for copy in loads:
        copy.wait()
    ones = jnp.ones((16, CHUNK * BLK), jnp.bfloat16)
    order = [
        (r, part * half + k) for part in range(2) for r in range(groups) for k in range(half)
    ]

    def tower_piece(m, step, slot):
        rows = pl.ds(m * (embed // TOWER_PIECES), embed // TOWER_PIECES)
        vectors = dot(tower_ref[rows, :], feat_s[lax.rem(step, RING)], NT)
        vec_s[slot, rows] = vectors.astype(jnp.bfloat16)

    def acc_piece(c, step, slot):
        cut = pl.ds(c * (features // ACC_PIECES), features // ACC_PIECES)
        acc[:, cut] += dot(grad_s[slot], feat_s[lax.rem(step, RING), :, cut])

    def prepare(step, unit):
        _, column, base = find(step, unit)
        slot = lax.rem(step, 2)
        vec = vec_s[slot, :, unit * BLK : (unit + 1) * BLK]
        vec_cat = jnp.concatenate([vec[b * H : (b + 1) * H] for b in range(K)], axis=1)
        near = [(r % CORES, r // CORES, column) for r in range(groups)]
        packed = jnp.concatenate([users_ref[at] for at in near], axis=0)
        vectors = jnp.concatenate([packed[:, :H], packed[:, H:]], axis=0)
        logit_s[unit] = dot(vectors, vec_cat)
        lines = jnp.concatenate([lines_ref[at] for at in near], axis=0)
        place = base + lax.broadcasted_iota(jnp.int32, (groups, BLK), 1)
        targets = []
        for k in range(users):
            hit = lines[:, k * picks : k * picks + 1] == place
            for p in range(k * picks + 1, (k + 1) * picks):
                hit = jnp.logical_or(hit, lines[:, p : p + 1] == place)
            targets.append(jnp.where(hit, 1.0, 0.0))
        return dict(
            unit=unit,
            slot=slot,
            column=column,
            valid=jnp.where(step * UNITS + unit < count, 1.0, 0.0),
            vec_cat=vec_cat,
            vectors=vectors,
            targets=targets,
            rows=[],
        )

    def chunk(state, first):
        unit = state["unit"]
        picked = range(first, first + CHUNK)
        logits = jnp.concatenate(
            [
                jnp.concatenate(
                    [
                        logit_s[unit, u * K : (u + 1) * K, b * BLK : (b + 1) * BLK]
                        for b in range(K)
                    ],
                    axis=0,
                )
                for u in picked
            ],
            axis=1,
        )
        wanted = jnp.concatenate(
            [state["targets"][order[u][1]][order[u][0] : order[u][0] + 1] for u in picked], axis=1
        )
        half_pre = dot(
            gin_t_ref[...], jnp.concatenate([logits.astype(jnp.bfloat16), ones], axis=0)
        )
        yield
        t = jnp.tanh(half_pre)
        up = 1.0 + t
        silu = half_pre * up
        slope = up + silu * (1.0 - t)
        gate = dot(gout_t_ref[...], jnp.concatenate([silu.astype(jnp.bfloat16), ones], axis=0))
        yield
        terms = jnp.exp(gate)
        mixture = terms * (1.0 / jnp.sum(terms, axis=0, keepdims=True))
        scores = jnp.sum(mixture * logits, axis=0, keepdims=True)
        score_grad = (0.5 + 0.5 * jnp.tanh(0.5 * scores) - wanted) * state["valid"]
        weighted = score_grad * mixture
        logit_grad = (weighted * (logits - scores)).astype(jnp.bfloat16)
        back = dot(gout_ref[...], logit_grad)
        yield
        hidden_grad = (back * slope).astype(jnp.bfloat16)
        more = dot(gin_ref[...], hidden_grad)
        yield
        pair = weighted + more
        for n in range(CHUNK):
            state["rows"].append(
                jnp.concatenate(
                    [
                        pair[b * K : (b + 1) * K, n * BLK : (n + 1) * BLK]
                        for b in range(K)
                    ],
                    axis=1,
                )
            )
        if len(state["rows"]) == column_users:
            pair_all = jnp.concatenate(state["rows"], axis=0).astype(jnp.bfloat16)
            uacc[state["column"]] += dot(pair_all, state["vec_cat"], NT)
            vectors_t = state["vectors"].astype(jnp.float32).T.astype(jnp.bfloat16)
            grad = dot(vectors_t, pair_all).astype(jnp.bfloat16)
            grad_s[state["slot"], :, unit * BLK : (unit + 1) * BLK] = jnp.concatenate(
                [grad[:, b * BLK : (b + 1) * BLK] for b in range(K)], axis=0
            )
        yield

    stages = 5

    def step_body(step, carry):
        @pl.when(step + 2 < steps)
        def _():
            for copy in fetch(step + 2):
                copy.start()

        @pl.when(step + 1 < steps)
        def _():
            for copy in fetch(step + 1):
                copy.wait()

        before = jnp.maximum(step - 1, 0)
        after = jnp.minimum(step + 1, steps - 1)
        other = lax.rem(step + 1, 2)
        extras = [functools.partial(tower_piece, m, after, other) for m in range(TOWER_PIECES)]
        extras += [functools.partial(acc_piece, c, before, other) for c in range(ACC_PIECES)]
        states = [prepare(step, unit) for unit in range(UNITS)]
        chunks = [
            chunk(state, first) for state in states for first in range(0, column_users, CHUNK)
        ]
        waves = len(chunks) + stages - 1
        done = 0
        for wave in range(waves):
            for n, work in enumerate(chunks):
                if 0 <= wave - n < stages:
                    next(work)
            while done < len(extras) * (wave + 1) // waves:
                extras[done]()
                done += 1
        return carry

    @pl.when(count > 0)
    def _():
        for copy in fetch(zero):
            copy.wait()
        for m in range(TOWER_PIECES):
            tower_piece(m, zero, 0)
        lax.fori_loop(0, steps, step_body, 0)
        for c in range(ACC_PIECES):
            acc_piece(c, steps - 1, lax.rem(steps - 1, 2))

    width = features // owners
    height = embed // groups
    share = half * K
    if width < LANES:
        out_ref[...] = jnp.zeros_like(out_ref)
    copies = []
    for d in range(owners):
        for r in range(groups):
            out_ref[d, r % CORES, r // CORES, 0:height, 0:width] = acc[
                r * height : (r + 1) * height, d * width : (d + 1) * width
            ].astype(jnp.bfloat16)
            parts = [
                uacc[d, (part * groups + r) * share : (part * groups + r + 1) * share]
                for part in range(2)
            ]
            out_ref[d, r % CORES, r // CORES, height : height + share, :] = (
                jnp.concatenate(parts, axis=1) * (1.0 / math.sqrt(H))
            ).astype(jnp.bfloat16)
        copy = pltpu.make_async_copy(out_ref.at[d], out_hbm.at[d], out_sem.at[d])
        copy.start()
        copies.append(copy)
    for copy in copies:
        copy.wait()


def sum_kernel(
    groups,
    owners,
    in_hbm,
    part_out,
    user_out,
    own,
    recv0,
    both,
    recv1,
    stage,
    recv2,
    part,
    final,
    own_sem,
    send0,
    rsem0,
    send1,
    rsem1,
    send2,
    rsem2,
    send3,
    rsem3,
):
    g = lax.axis_index("blk")
    s = lax.axis_index("shard")
    height = part.shape[0]
    chips = groups // CORES
    core = lax.rem(g, CORES)
    chip = g // CORES
    sister = chip * CORES + (CORES - 1) - core

    def peer(d):
        if owners & (owners - 1):
            return lax.rem(s + d, owners)
        to = s
        bit = 1
        while bit < owners:
            if d & bit:
                to = to + bit * (1 - 2 * lax.rem(s // bit, 2))
            bit *= 2
        return to

    barrier = pltpu.get_barrier_semaphore()
    for d in range(1, groups):
        pl.semaphore_signal(
            barrier, inc=1, device_id=(lax.rem(g + d, groups), s), device_id_type=MESH
        )
    for d in range(1, owners):
        pl.semaphore_signal(barrier, inc=1, device_id=(g, peer(d)), device_id_type=MESH)
    local = pltpu.make_async_copy(in_hbm.at[:, core], own, own_sem)
    local.start()
    pl.semaphore_wait(barrier, groups + owners - 2)

    order = list(range(owners - 1, -1, -1))
    first = []
    for n, d in enumerate(order):
        copy = pltpu.make_async_remote_copy(
            src_ref=in_hbm.at[peer(d), CORES - 1 - core], dst_ref=recv0.at[n],
            send_sem=send0.at[n], recv_sem=rsem0.at[n],
            device_id=(sister, s), device_id_type=MESH,
        )
        copy.start()
        first.append(copy)
    local.wait()
    second = []
    for n, d in enumerate(order):
        first[n].wait()
        second.append([])
        for c in range(1, chips):
            to = lax.rem(chip + c, chips)
            both[n, c - 1] = (
                own[peer(d), to].astype(jnp.float32) + recv0[n, to].astype(jnp.float32)
            ).astype(jnp.bfloat16)
            copy = pltpu.make_async_remote_copy(
                src_ref=both.at[n, c - 1], dst_ref=recv1.at[n, c - 1],
                send_sem=send1.at[n, c - 1], recv_sem=rsem1.at[n, c - 1],
                device_id=(to * CORES + core, s), device_id_type=MESH,
            )
            copy.start()
            second[n].append(copy)
    third = []
    total = None
    for n, d in enumerate(order):
        for copy in second[n]:
            copy.wait()
        total = own[peer(d), chip].astype(jnp.float32) + recv0[n, chip].astype(jnp.float32)
        for c in range(1, chips):
            total = total + recv1[n, c - 1].astype(jnp.float32)
        if d:
            stage[n] = total.astype(jnp.bfloat16)
            copy = pltpu.make_async_remote_copy(
                src_ref=stage.at[n], dst_ref=recv2.at[n],
                send_sem=send2.at[n], recv_sem=rsem2.at[n],
                device_id=(g, peer(d)), device_id_type=MESH,
            )
            copy.start()
            third.append(copy)
    for n, copy in enumerate(third):
        copy.wait()
        total = total + recv2[n].astype(jnp.float32)
    user_out[...] = total[height:]
    part[...] = total[:height].astype(jnp.bfloat16)

    copies = []
    for d in range(1, groups):
        copy = pltpu.make_async_remote_copy(
            src_ref=part, dst_ref=final.at[g],
            send_sem=send3.at[d - 1], recv_sem=rsem3.at[d - 1],
            device_id=(lax.rem(g + d, groups), s), device_id_type=MESH,
        )
        copy.start()
        copies.append(copy)
    final[g] = part[...]
    for copy in copies:
        copy.wait()
    part_out[...] = final[...]


def finish_kernel(users, ids_ref, part_ref, user_ref, tower_out, user_out):
    groups, height, _ = part_ref.shape
    width = tower_out.shape[0]
    for r in range(groups):
        tower_out[:, r * height : (r + 1) * height] = part_ref[r].astype(jnp.float32).T[:width]
    half = users // 2
    straight = user_ref[...]
    turned = pltpu.roll(straight, H, 1)
    table, embed = user_out.shape
    row = lax.broadcasted_iota(jnp.int32, (table, LANES), 0)
    low = lax.broadcasted_iota(jnp.int32, (1, LANES), 1) < H
    for first in range(0, embed, LANES):
        total = jnp.zeros((table, LANES), jnp.float32)
        for k in range(users):
            at = (k % half) * K + first // H
            left, right = (straight, turned) if k < half else (turned, straight)
            line = jnp.where(low, left[at : at + 1], right[at + 1 : at + 2])
            total = total + jnp.where(row == ids_ref[k], line, 0.0)
        user_out[:, first : first + LANES] = total


def shards(
    item_features,
    tower_weight,
    gate_in,
    gate_in_bias,
    gate_out,
    gate_out_bias,
    user_table,
    user_ids,
    positive_item,
    listed_owner,
    listed_slot,
):
    groups = lax.axis_size("blk")
    owners = lax.axis_size("shard")
    chips = groups // CORES
    trainers = groups * owners
    listings = listed_slot.shape[0]
    users, picks = positive_item.shape
    table = user_table.shape[0]
    features = item_features.shape[1]
    embed = tower_weight.shape[1]
    hidden = gate_in.shape[1]
    pairs = K * K
    rows = groups * users * K
    share = users // 2 * K
    bf16, f32, i32 = jnp.bfloat16, jnp.float32, jnp.int32
    vmem = pl.BlockSpec(memory_space=pltpu.VMEM)
    smem = pl.BlockSpec(memory_space=pltpu.SMEM)
    hbm = pl.BlockSpec(memory_space=pl.ANY)
    dma = pltpu.SemaphoreType.DMA
    partners = chips * owners - 1

    all_users, all_lines, gin, gin_t, gout, gout_t, tower_t = pl.pallas_call(
        functools.partial(gather_kernel, groups, owners),
        out_shape=(
            jax.ShapeDtypeStruct((CORES, chips, owners, share, LANES), bf16),
            jax.ShapeDtypeStruct((CORES, chips, owners, 1, LANES), i32),
            jax.ShapeDtypeStruct((pairs, hidden), bf16),
            jax.ShapeDtypeStruct((hidden, pairs + 16), bf16),
            jax.ShapeDtypeStruct((hidden, pairs), bf16),
            jax.ShapeDtypeStruct((pairs, hidden + 16), bf16),
            jax.ShapeDtypeStruct((embed, features), bf16),
        ),
        in_specs=[hbm] * 10,
        out_specs=(vmem,) * 7,
        scratch_shapes=[
            pltpu.VMEM((CORES, chips, owners, share, LANES), bf16),
            pltpu.VMEM((CORES, chips, owners, 1, LANES), i32),
            pltpu.SMEM((users,), i32),
            pltpu.SMEM((users, picks), i32),
            pltpu.SMEM((1, listings), i32),
            pltpu.SMEM((listings,), i32),
            pltpu.VMEM((table, embed), bf16),
            pltpu.VMEM((pairs, hidden), bf16),
            pltpu.VMEM((1, hidden), bf16),
            pltpu.VMEM((pairs, hidden), bf16),
            pltpu.VMEM((1, pairs), bf16),
            pltpu.VMEM((features, embed), bf16),
            dma((10,)),
            dma((2, partners)),
            dma((2, partners)),
            dma((2,)),
            dma((2,)),
        ],
        compiler_params=pltpu.CompilerParams(collective_id=1, has_side_effects=True),
        name="gather_users",
    )(
        user_ids,
        positive_item,
        listed_owner.T,
        listed_slot,
        user_table,
        gate_in,
        gate_in_bias[None, :],
        gate_out.T,
        gate_out_bias[None, :],
        tower_weight,
    )

    most = trainers * min(CAP, listings)
    height = embed // groups
    width = features // owners
    terms = pl.pallas_call(
        functools.partial(pair_kernel, groups, owners, users, picks, listings),
        out_shape=jax.ShapeDtypeStruct((owners, CORES, chips, height + share, LANES), bf16),
        in_specs=[smem] + [hbm] * 8,
        out_specs=hbm,
        scratch_shapes=[
            pltpu.VMEM((CORES, chips, owners, share, LANES), bf16),
            pltpu.VMEM((CORES, chips, owners, 1, LANES), i32),
            pltpu.VMEM((pairs, hidden), bf16),
            pltpu.VMEM((hidden, pairs + 16), bf16),
            pltpu.VMEM((hidden, pairs), bf16),
            pltpu.VMEM((pairs, hidden + 16), bf16),
            pltpu.VMEM((embed, features), bf16),
            pltpu.VMEM((owners, CORES, chips, height + share, LANES), bf16),
            pltpu.VMEM((embed, features), f32),
            pltpu.VMEM((owners, rows, H), f32),
            pltpu.VMEM((UNITS, rows, K * BLK), f32),
            pltpu.VMEM((RING, UNITS * BLK, features), bf16),
            pltpu.VMEM((2, embed, UNITS * BLK), bf16),
            pltpu.VMEM((2, embed, UNITS * BLK), bf16),
            dma((RING, UNITS)),
            dma((7,)),
            dma((owners,)),
            pltpu.SMEM((most + 1,), i32),
        ],
        compiler_params=pltpu.CompilerParams(vmem_limit_bytes=32 << 20),
        name="pair_terms",
    )(
        all_lines.reshape(trainers, 1, LANES),
        item_features,
        all_users,
        all_lines,
        gin,
        gin_t,
        gout,
        gout_t,
        tower_t,
    )

    block = (height + share, LANES)
    part, user_terms = pl.pallas_call(
        functools.partial(sum_kernel, groups, owners),
        out_shape=(
            jax.ShapeDtypeStruct((groups, height, LANES), bf16),
            jax.ShapeDtypeStruct((share, LANES), f32),
        ),
        in_specs=[hbm],
        out_specs=(vmem, vmem),
        scratch_shapes=[
            pltpu.VMEM((owners, chips) + block, bf16),
            pltpu.VMEM((owners, chips) + block, bf16),
            pltpu.VMEM((owners, chips - 1) + block, bf16),
            pltpu.VMEM((owners, chips - 1) + block, bf16),
            pltpu.VMEM((owners - 1,) + block, bf16),
            pltpu.VMEM((owners - 1,) + block, bf16),
            pltpu.VMEM((height, LANES), bf16),
            pltpu.VMEM((groups, height, LANES), bf16),
            dma,
            dma((owners,)),
            dma((owners,)),
            dma((owners, chips - 1)),
            dma((owners, chips - 1)),
            dma((owners - 1,)),
            dma((owners - 1,)),
            dma((groups - 1,)),
            dma((groups - 1,)),
        ],
        compiler_params=pltpu.CompilerParams(collective_id=0, has_side_effects=True),
        name="sum_terms",
    )(terms)

    return pl.pallas_call(
        functools.partial(finish_kernel, users),
        out_shape=(
            jax.ShapeDtypeStruct((width, embed), f32),
            jax.ShapeDtypeStruct((table, embed), f32),
        ),
        in_specs=[smem, vmem, vmem],
        out_specs=(vmem, vmem),
        name="finish",
    )(user_ids, part, user_terms)


def solution(mesh):
    return jax.shard_map(
        shards,
        mesh=mesh,
        in_specs=(
            P("shard", None),
            P(),
            P(),
            P(),
            P(),
            P(),
            P(("blk", "shard"), None),
            P(("blk", "shard")),
            P(("blk", "shard"), None),
            P(("blk", "shard"), None),
            P(("blk", "shard")),
        ),
        out_specs=(P("shard", None), P(("blk", "shard"), None)),
        check_vma=False,
    )
```

```python
import functools
import math

import jax
import jax.numpy as jnp
from jax import lax
from jax.experimental import pallas as pl
from jax.experimental.pallas import tpu as pltpu
from jax.sharding import PartitionSpec as P

K = 8
H = 64
BLK = 128
CAP = 2
LANES = 128
CORES = 2
UNITS = 2
CHUNK = 8
TOWER_PIECES = 2
ACC_PIECES = 4
RING = 4
SCAN_ROWS = 4

NN = (((1,), (0,)), ((), ()))
NT = (((1,), (1,)), ((), ()))
MESH = pl.DeviceIdType.MESH


def dot(left, right, dims=NN):
    return lax.dot_general(left, right, dims, preferred_element_type=jnp.float32)


def gather_kernel(
    groups,
    owners,
    ids_hbm,
    pos_hbm,
    owner_hbm,
    slot_hbm,
    table_hbm,
    gin_hbm,
    gin_b_hbm,
    gout_hbm,
    gout_b_hbm,
    tower_hbm,
    users_out,
    lines_out,
    gin_ref,
    gin_t_ref,
    gout_ref,
    gout_t_ref,
    tower_t_ref,
    users,
    lines,
    ids_ref,
    pos_ref,
    owner_ref,
    slot_ref,
    table_ref,
    gin_in,
    gin_b_in,
    gout_in,
    gout_b_in,
    tower_s,
    load_sem,
    send1,
    recv1,
    send2,
    recv2,
):
    g = lax.axis_index("blk")
    s = lax.axis_index("shard")
    chips = groups // CORES
    core = lax.rem(g, CORES)
    chip = g // CORES
    sister = chip * CORES + (CORES - 1) - core
    partners = [(c, d) for c in range(chips) for d in range(owners) if c or d]

    def device(c, d):
        return (lax.rem(chip + c, chips) * CORES + core, lax.rem(s + d, owners))

    barrier = pltpu.get_barrier_semaphore()
    for c, d in partners:
        pl.semaphore_signal(barrier, inc=1, device_id=device(c, d), device_id_type=MESH)
    pl.semaphore_signal(barrier, inc=1, device_id=(sister, s), device_id_type=MESH)
    loads = [
        pltpu.make_async_copy(source, to, load_sem.at[n])
        for n, (source, to) in enumerate(
            (
                (ids_hbm, ids_ref),
                (pos_hbm, pos_ref),
                (owner_hbm, owner_ref),
                (slot_hbm, slot_ref),
                (table_hbm, table_ref),
                (gin_hbm, gin_in),
                (gin_b_hbm, gin_b_in),
                (gout_hbm, gout_in),
                (gout_b_hbm, gout_b_in),
                (tower_hbm, tower_s),
            )
        )
    ]
    for copy in loads:
        copy.start()
    for copy in loads[:5]:
        copy.wait()

    count, picks = pos_ref.shape
    listings = slot_ref.shape[0]
    half = count // 2
    table, embed = table_ref.shape
    rows = half * K
    row = lax.broadcasted_iota(jnp.int32, (rows, table), 0)
    column = lax.broadcasted_iota(jnp.int32, (rows, table), 1)
    block = lax.broadcasted_iota(jnp.int32, (rows, embed), 1) // H
    mine = block == lax.broadcasted_iota(jnp.int32, (rows, embed), 0) % K
    parts = []
    for part in range(2):
        wanted = jnp.zeros((rows, table), jnp.int32)
        for k in range(half):
            wanted = jnp.where(row // K == k, ids_ref[part * half + k], wanted)
        picked = dot(jnp.where(column == wanted, 1.0, 0.0).astype(jnp.bfloat16), table_ref[...])
        picked = jnp.where(mine, picked * (1.0 / math.sqrt(H)), 0.0)
        total = picked[:, :LANES]
        for first in range(LANES, embed, LANES):
            total = total + picked[:, first : first + LANES]
        parts.append(total + pltpu.roll(total, H, 1))
    lane = lax.broadcasted_iota(jnp.int32, (rows, LANES), 1)
    users[core, chip, s] = jnp.where(lane < H, parts[0], parts[1]).astype(jnp.bfloat16)
    lane = lax.broadcasted_iota(jnp.int32, (1, LANES), 1)
    line = jnp.zeros((1, LANES), jnp.int32)
    for k in range(count):
        for p in range(picks):
            line = jnp.where(lane == k * picks + p, pos_ref[k, p], line)
    for j in range(listings):
        line = jnp.where(lane == count * picks + j, owner_ref[0, j], line)
        line = jnp.where(lane == count * picks + listings + j, slot_ref[j], line)
    lines[core, chip, s] = line

    pl.semaphore_wait(barrier, len(partners) + 1)
    copies = []
    for n, (c, d) in enumerate(partners):
        for m, ref in enumerate((users, lines)):
            copy = pltpu.make_async_remote_copy(
                src_ref=ref.at[core, chip, s], dst_ref=ref.at[core, chip, s],
                send_sem=send1.at[m, n], recv_sem=recv1.at[m, n],
                device_id=device(c, d), device_id_type=MESH,
            )
            copy.start()
            copies.append(copy)
    for copy in loads[5:]:
        copy.wait()
    tower_t_ref[...] = tower_s[...].T
    pairs, hidden = gin_in.shape
    to = lax.broadcasted_iota(jnp.int32, (pairs, pairs), 0)
    of = lax.broadcasted_iota(jnp.int32, (pairs, pairs), 1)
    turn = jnp.where(of == (to % K) * K + to // K, 1.0, 0.0).astype(jnp.bfloat16)

    def beside(row, scale):
        column = jnp.broadcast_to(row.astype(jnp.float32), (LANES, row.shape[1])).T[:, :16]
        lane = lax.broadcasted_iota(jnp.int32, column.shape, 1)
        return jnp.where(lane == 0, column * scale, 0.0).astype(jnp.bfloat16)

    gin = dot(turn, gin_in[...])
    gin_ref[...] = gin.astype(jnp.bfloat16)
    gin_t_ref[:, :pairs] = (0.5 * gin.T).astype(jnp.bfloat16)
    gin_t_ref[:, pairs:] = beside(gin_b_in[...], 0.5)
    gout_t = dot(turn, gout_in[...])
    gout_ref[...] = (0.5 * gout_t.T).astype(jnp.bfloat16)
    gout_t_ref[:, :hidden] = gout_t.astype(jnp.bfloat16)
    gout_t_ref[:, hidden:] = dot(turn, beside(gout_b_in[...], 1.0)).astype(jnp.bfloat16)
    for copy in copies:
        copy.wait()
    copies = []
    for m, ref in enumerate((users, lines)):
        copy = pltpu.make_async_remote_copy(
            src_ref=ref.at[core], dst_ref=ref.at[core],
            send_sem=send2.at[m], recv_sem=recv2.at[m],
            device_id=(sister, s), device_id_type=MESH,
        )
        copy.start()
        copies.append(copy)
    for copy in copies:
        copy.wait()
    users_out[...] = users[...]
    lines_out[...] = lines[...]


def pair_kernel(
    groups,
    owners,
    users,
    picks,
    listings,
    lists_ref,
    feat_hbm,
    users_hbm,
    lines_hbm,
    gin_hbm,
    gin_t_hbm,
    gout_hbm,
    gout_t_hbm,
    tower_hbm,
    out_hbm,
    users_ref,
    lines_ref,
    gin_ref,
    gin_t_ref,
    gout_ref,
    gout_t_ref,
    tower_ref,
    out_ref,
    acc,
    uacc,
    logit_s,
    feat_s,
    vec_s,
    grad_s,
    feat_sem,
    load_sem,
    out_sem,
    entries,
):
    g = lax.axis_index("blk")
    s = lax.axis_index("shard")
    chips = groups // CORES
    column_users = groups * users
    half = users // 2
    embed, features = tower_ref.shape
    first_owner = users * picks

    loads = [
        pltpu.make_async_copy(source, to, load_sem.at[n])
        for n, (source, to) in enumerate(
            (
                (tower_hbm, tower_ref),
                (users_hbm, users_ref),
                (lines_hbm, lines_ref),
                (gin_hbm, gin_ref),
                (gin_t_hbm, gin_t_ref),
                (gout_hbm, gout_ref),
                (gout_t_hbm, gout_t_ref),
            )
        )
    ]
    for copy in loads:
        copy.start()

    def scan(turn, n):
        for row in range(SCAN_ROWS):
            for j in range(listings):
                entries[n] = (turn * SCAN_ROWS + row) * listings + j
                mine = lists_ref[turn * SCAN_ROWS + row, 0, first_owner + j] == s
                n = n + mine.astype(jnp.int32)
        return n

    zero = jnp.int32(0)
    listed = lax.fori_loop(0, groups * owners // SCAN_ROWS, scan, zero)
    count = (listed + groups - 1 - g) // groups
    steps = (count + UNITS - 1) // UNITS

    def find(step, unit):
        n = jnp.minimum(step * UNITS + unit, count - 1)
        entry = entries[n * groups + g]
        row = entry // listings
        j = entry - row * listings
        place = row // owners
        group = lax.rem(place, chips) * CORES + place // chips
        slot = lists_ref[row, 0, first_owner + listings + j]
        return slot, lax.rem(row, owners), (group * listings + j) * BLK

    def fetch(step):
        copies = []
        for j in range(UNITS):
            block, _, _ = find(step, j)
            copies.append(
                pltpu.make_async_copy(
                    feat_hbm.at[pl.ds(pl.multiple_of(block * BLK, BLK), BLK)],
                    feat_s.at[lax.rem(step, RING), pl.ds(j * BLK, BLK)],
                    feat_sem.at[lax.rem(step, RING), j],
                )
            )
        return copies

    @pl.when(count > 0)
    def _():
        for copy in fetch(zero):
            copy.start()

    @pl.when(steps > 1)
    def _():
        for copy in fetch(zero + 1):
            copy.start()

    acc[...] = jnp.zeros_like(acc)
    uacc[...] = jnp.zeros_like(uacc)
    grad_s[...] = jnp.zeros_like(grad_s)

    @pl.when(count == 0)
    def _():
        feat_s[0] = jnp.zeros(feat_s.shape[1:], feat_s.dtype)

    for copy in loads:
        copy.wait()
    ones = jnp.ones((16, CHUNK * BLK), jnp.bfloat16)
    order = [
        (r, part * half + k) for part in range(2) for r in range(groups) for k in range(half)
    ]

    def tower_piece(m, step, slot):
        rows = pl.ds(m * (embed // TOWER_PIECES), embed // TOWER_PIECES)
        vectors = dot(tower_ref[rows, :], feat_s[lax.rem(step, RING)], NT)
        vec_s[slot, rows] = vectors.astype(jnp.bfloat16)

    def acc_piece(c, step, slot):
        cut = pl.ds(c * (features // ACC_PIECES), features // ACC_PIECES)
        acc[:, cut] += dot(grad_s[slot], feat_s[lax.rem(step, RING), :, cut])

    def prepare(step, unit):
        _, column, base = find(step, unit)
        slot = lax.rem(step, 2)
        vec = vec_s[slot, :, unit * BLK : (unit + 1) * BLK]
        vec_cat = jnp.concatenate([vec[b * H : (b + 1) * H] for b in range(K)], axis=1)
        near = [(r % CORES, r // CORES, column) for r in range(groups)]
        packed = jnp.concatenate([users_ref[at] for at in near], axis=0)
        vectors = jnp.concatenate([packed[:, :H], packed[:, H:]], axis=0)
        logit_s[unit] = dot(vectors, vec_cat)
        lines = jnp.concatenate([lines_ref[at] for at in near], axis=0)
        place = base + lax.broadcasted_iota(jnp.int32, (groups, BLK), 1)
        targets = []
        for k in range(users):
            hit = lines[:, k * picks : k * picks + 1] == place
            for p in range(k * picks + 1, (k + 1) * picks):
                hit = jnp.logical_or(hit, lines[:, p : p + 1] == place)
            targets.append(jnp.where(hit, 1.0, 0.0))
        return dict(
            unit=unit,
            slot=slot,
            column=column,
            valid=jnp.where(step * UNITS + unit < count, 1.0, 0.0),
            vec_cat=vec_cat,
            vectors=vectors,
            targets=targets,
            rows=[],
        )

    def chunk(state, first):
        unit = state["unit"]
        picked = range(first, first + CHUNK)
        logits = jnp.concatenate(
            [
                jnp.concatenate(
                    [
                        logit_s[unit, u * K : (u + 1) * K, b * BLK : (b + 1) * BLK]
                        for b in range(K)
                    ],
                    axis=0,
                )
                for u in picked
            ],
            axis=1,
        )
        wanted = jnp.concatenate(
            [state["targets"][order[u][1]][order[u][0] : order[u][0] + 1] for u in picked], axis=1
        )
        half_pre = dot(
            gin_t_ref[...], jnp.concatenate([logits.astype(jnp.bfloat16), ones], axis=0)
        )
        yield
        t = jnp.tanh(half_pre)
        up = 1.0 + t
        silu = half_pre * up
        slope = up + silu * (1.0 - t)
        gate = dot(gout_t_ref[...], jnp.concatenate([silu.astype(jnp.bfloat16), ones], axis=0))
        yield
        terms = jnp.exp(gate)
        mixture = terms * (1.0 / jnp.sum(terms, axis=0, keepdims=True))
        scores = jnp.sum(mixture * logits, axis=0, keepdims=True)
        score_grad = (0.5 + 0.5 * jnp.tanh(0.5 * scores) - wanted) * state["valid"]
        weighted = score_grad * mixture
        logit_grad = (weighted * (logits - scores)).astype(jnp.bfloat16)
        back = dot(gout_ref[...], logit_grad)
        yield
        hidden_grad = (back * slope).astype(jnp.bfloat16)
        more = dot(gin_ref[...], hidden_grad)
        yield
        pair = weighted + more
        for n in range(CHUNK):
            state["rows"].append(
                jnp.concatenate(
                    [
                        pair[b * K : (b + 1) * K, n * BLK : (n + 1) * BLK]
                        for b in range(K)
                    ],
                    axis=1,
                )
            )
        if len(state["rows"]) == column_users:
            pair_all = jnp.concatenate(state["rows"], axis=0).astype(jnp.bfloat16)
            uacc[state["column"]] += dot(pair_all, state["vec_cat"], NT)
            vectors_t = state["vectors"].astype(jnp.float32).T.astype(jnp.bfloat16)
            grad = dot(vectors_t, pair_all).astype(jnp.bfloat16)
            grad_s[state["slot"], :, unit * BLK : (unit + 1) * BLK] = jnp.concatenate(
                [grad[:, b * BLK : (b + 1) * BLK] for b in range(K)], axis=0
            )
        yield

    stages = 5

    def step_body(step, carry):
        @pl.when(step + 2 < steps)
        def _():
            for copy in fetch(step + 2):
                copy.start()

        @pl.when(step + 1 < steps)
        def _():
            for copy in fetch(step + 1):
                copy.wait()

        before = jnp.maximum(step - 1, 0)
        after = jnp.minimum(step + 1, steps - 1)
        other = lax.rem(step + 1, 2)
        extras = [functools.partial(tower_piece, m, after, other) for m in range(TOWER_PIECES)]
        extras += [functools.partial(acc_piece, c, before, other) for c in range(ACC_PIECES)]
        states = [prepare(step, unit) for unit in range(UNITS)]
        chunks = [
            chunk(state, first) for state in states for first in range(0, column_users, CHUNK)
        ]
        waves = len(chunks) + stages - 1
        done = 0
        for wave in range(waves):
            for n, work in enumerate(chunks):
                if 0 <= wave - n < stages:
                    next(work)
            while done < len(extras) * (wave + 1) // waves:
                extras[done]()
                done += 1
        return carry

    @pl.when(count > 0)
    def _():
        for copy in fetch(zero):
            copy.wait()
        for m in range(TOWER_PIECES):
            tower_piece(m, zero, 0)
        lax.fori_loop(0, steps, step_body, 0)

    width = features // owners
    height = embed // groups
    share = half * K
    cut = features // ACC_PIECES
    last = jnp.maximum(steps - 1, 0)
    if width < LANES:
        out_ref[...] = jnp.zeros_like(out_ref)
    for d in range(owners):
        for r in range(groups):
            parts = [
                uacc[d, (part * groups + r) * share : (part * groups + r + 1) * share]
                for part in range(2)
            ]
            out_ref[d, r % CORES, r // CORES, height : height + share, :] = (
                jnp.concatenate(parts, axis=1) * (1.0 / math.sqrt(H))
            ).astype(jnp.bfloat16)
    copies = []
    for c in range(ACC_PIECES):
        at = slice(c * cut, (c + 1) * cut)
        block = acc[:, at] + dot(grad_s[lax.rem(last, 2)], feat_s[lax.rem(last, RING), :, at])
        block = block.astype(jnp.bfloat16)
        for d in range(c * cut // width, (c + 1) * cut // width):
            for r in range(groups):
                first = d * width - c * cut
                out_ref[d, r % CORES, r // CORES, 0:height, 0:width] = block[
                    r * height : (r + 1) * height, first : first + width
                ]
            copy = pltpu.make_async_copy(out_ref.at[d], out_hbm.at[d], out_sem.at[d])
            copy.start()
            copies.append(copy)
    for copy in copies:
        copy.wait()


def sum_kernel(
    groups,
    owners,
    in_hbm,
    part_out,
    user_out,
    own,
    recv0,
    both,
    recv1,
    stage,
    recv2,
    part,
    final,
    own_sem,
    send0,
    rsem0,
    send1,
    rsem1,
    send2,
    rsem2,
    send3,
    rsem3,
):
    g = lax.axis_index("blk")
    s = lax.axis_index("shard")
    height = part.shape[0]
    core = lax.rem(g, CORES)
    chip = g // CORES
    sister = chip * CORES + (CORES - 1) - core

    def pick(zero, one):
        return zero * (1 - core) + one * core

    def flip(value, bits):
        to = value
        bit = 1
        while bit <= bits:
            if bits & bit:
                to = to + bit * (1 - 2 * lax.rem(value // bit, 2))
            bit *= 2
        return to

    def mine(n):
        return (
            pick(chip, flip(chip, n & 1)),
            pick(flip(s, n), flip(s, n & ~1)),
            pick(n, n & ~1),
        )

    def other(n):
        return (
            pick(flip(chip, 1), flip(chip, n & 1)),
            pick(flip(s, n), flip(s, n | 1)),
            pick(n, n | 1),
        )

    partner = (pick(flip(chip, 1), chip) * CORES + core, pick(s, flip(s, 1)))
    barrier = pltpu.get_barrier_semaphore()
    for d in range(1, groups):
        pl.semaphore_signal(
            barrier, inc=1, device_id=(lax.rem(g + d, groups), s), device_id_type=MESH
        )
    for n in range(1, owners):
        to = (g, flip(s, 1))
        if n > 1:
            at = mine(n)
            to = (at[0] * CORES + core, at[1])
        pl.semaphore_signal(barrier, inc=1, device_id=to, device_id_type=MESH)
    local = pltpu.make_async_copy(in_hbm.at[:, core], own, own_sem)
    local.start()
    pl.semaphore_wait(barrier, groups + owners - 2)

    order = list(range(owners - 1, -1, -1))
    first = {}
    for d in order:
        first[d] = pltpu.make_async_remote_copy(
            src_ref=in_hbm.at[flip(s, d), CORES - 1 - core], dst_ref=recv0.at[d],
            send_sem=send0.at[d], recv_sem=rsem0.at[d],
            device_id=(sister, s), device_id_type=MESH,
        )
        first[d].start()
    local.wait()

    def summed(at):
        c, d, n = at
        return own[d, c].astype(jnp.float32) + recv0[n, c].astype(jnp.float32)

    second = {}
    for n in order:
        if n % 2:
            first[n].wait()
            first[n - 1].wait()
        both[n] = summed(other(n)).astype(jnp.bfloat16)
        second[n] = pltpu.make_async_remote_copy(
            src_ref=both.at[n], dst_ref=recv1.at[n],
            send_sem=send1.at[n], recv_sem=rsem1.at[n],
            device_id=partner, device_id_type=MESH,
        )
        second[n].start()
    third = []
    total = None
    for n in order:
        second[n].wait()
        total = summed(mine(n)) + recv1[n].astype(jnp.float32)
        if n:
            stage[n - 1] = total.astype(jnp.bfloat16)
            at = mine(n)
            copy = pltpu.make_async_remote_copy(
                src_ref=stage.at[n - 1], dst_ref=recv2.at[n - 1],
                send_sem=send2.at[n - 1], recv_sem=rsem2.at[n - 1],
                device_id=(at[0] * CORES + core, at[1]), device_id_type=MESH,
            )
            copy.start()
            third.append((n - 1, copy))
    for n, copy in third:
        copy.wait()
        total = total + recv2[n].astype(jnp.float32)
    user_out[...] = total[height:]
    part[...] = total[:height].astype(jnp.bfloat16)

    copies = []
    for d in range(1, groups):
        copy = pltpu.make_async_remote_copy(
            src_ref=part, dst_ref=final.at[g],
            send_sem=send3.at[d - 1], recv_sem=rsem3.at[d - 1],
            device_id=(lax.rem(g + d, groups), s), device_id_type=MESH,
        )
        copy.start()
        copies.append(copy)
    final[g] = part[...]
    for copy in copies:
        copy.wait()
    part_out[...] = final[...]


def finish_kernel(
    users, ids_ref, part_ref, user_ref, tower_hbm, user_hbm, tower_out, user_out, sems
):
    groups, height, _ = part_ref.shape
    width = tower_out.shape[0]
    for r in range(groups):
        tower_out[:, r * height : (r + 1) * height] = part_ref[r].astype(jnp.float32).T[:width]
    tower = pltpu.make_async_copy(tower_out, tower_hbm, sems.at[0])
    tower.start()
    half = users // 2
    straight = user_ref[...]
    turned = pltpu.roll(straight, H, 1)
    table, embed = user_out.shape
    row = lax.broadcasted_iota(jnp.int32, (table, LANES), 0)
    low = lax.broadcasted_iota(jnp.int32, (1, LANES), 1) < H
    for first in range(0, embed, LANES):
        total = jnp.zeros((table, LANES), jnp.float32)
        for k in range(users):
            at = (k % half) * K + first // H
            left, right = (straight, turned) if k < half else (turned, straight)
            line = jnp.where(low, left[at : at + 1], right[at + 1 : at + 2])
            total = total + jnp.where(row == ids_ref[k], line, 0.0)
        user_out[:, first : first + LANES] = total
    user = pltpu.make_async_copy(user_out, user_hbm, sems.at[1])
    user.start()
    tower.wait()
    user.wait()


def shards(
    item_features,
    tower_weight,
    gate_in,
    gate_in_bias,
    gate_out,
    gate_out_bias,
    user_table,
    user_ids,
    positive_item,
    listed_owner,
    listed_slot,
):
    groups = lax.axis_size("blk")
    owners = lax.axis_size("shard")
    chips = groups // CORES
    trainers = groups * owners
    listings = listed_slot.shape[0]
    users, picks = positive_item.shape
    table = user_table.shape[0]
    features = item_features.shape[1]
    embed = tower_weight.shape[1]
    hidden = gate_in.shape[1]
    pairs = K * K
    rows = groups * users * K
    share = users // 2 * K
    bf16, f32, i32 = jnp.bfloat16, jnp.float32, jnp.int32
    vmem = pl.BlockSpec(memory_space=pltpu.VMEM)
    smem = pl.BlockSpec(memory_space=pltpu.SMEM)
    hbm = pl.BlockSpec(memory_space=pl.ANY)
    dma = pltpu.SemaphoreType.DMA
    partners = chips * owners - 1

    all_users, all_lines, gin, gin_t, gout, gout_t, tower_t = pl.pallas_call(
        functools.partial(gather_kernel, groups, owners),
        out_shape=(
            jax.ShapeDtypeStruct((CORES, chips, owners, share, LANES), bf16),
            jax.ShapeDtypeStruct((CORES, chips, owners, 1, LANES), i32),
            jax.ShapeDtypeStruct((pairs, hidden), bf16),
            jax.ShapeDtypeStruct((hidden, pairs + 16), bf16),
            jax.ShapeDtypeStruct((hidden, pairs), bf16),
            jax.ShapeDtypeStruct((pairs, hidden + 16), bf16),
            jax.ShapeDtypeStruct((embed, features), bf16),
        ),
        in_specs=[hbm] * 10,
        out_specs=(vmem,) * 7,
        scratch_shapes=[
            pltpu.VMEM((CORES, chips, owners, share, LANES), bf16),
            pltpu.VMEM((CORES, chips, owners, 1, LANES), i32),
            pltpu.SMEM((users,), i32),
            pltpu.SMEM((users, picks), i32),
            pltpu.SMEM((1, listings), i32),
            pltpu.SMEM((listings,), i32),
            pltpu.VMEM((table, embed), bf16),
            pltpu.VMEM((pairs, hidden), bf16),
            pltpu.VMEM((1, hidden), bf16),
            pltpu.VMEM((pairs, hidden), bf16),
            pltpu.VMEM((1, pairs), bf16),
            pltpu.VMEM((features, embed), bf16),
            dma((10,)),
            dma((2, partners)),
            dma((2, partners)),
            dma((2,)),
            dma((2,)),
        ],
        compiler_params=pltpu.CompilerParams(collective_id=1, has_side_effects=True),
        name="gather_users",
    )(
        user_ids,
        positive_item,
        listed_owner.T,
        listed_slot,
        user_table,
        gate_in,
        gate_in_bias[None, :],
        gate_out.T,
        gate_out_bias[None, :],
        tower_weight,
    )

    most = trainers * min(CAP, listings)
    height = embed // groups
    width = features // owners
    terms = pl.pallas_call(
        functools.partial(pair_kernel, groups, owners, users, picks, listings),
        out_shape=jax.ShapeDtypeStruct((owners, CORES, chips, height + share, LANES), bf16),
        in_specs=[smem] + [hbm] * 8,
        out_specs=hbm,
        scratch_shapes=[
            pltpu.VMEM((CORES, chips, owners, share, LANES), bf16),
            pltpu.VMEM((CORES, chips, owners, 1, LANES), i32),
            pltpu.VMEM((pairs, hidden), bf16),
            pltpu.VMEM((hidden, pairs + 16), bf16),
            pltpu.VMEM((hidden, pairs), bf16),
            pltpu.VMEM((pairs, hidden + 16), bf16),
            pltpu.VMEM((embed, features), bf16),
            pltpu.VMEM((owners, CORES, chips, height + share, LANES), bf16),
            pltpu.VMEM((embed, features), f32),
            pltpu.VMEM((owners, rows, H), f32),
            pltpu.VMEM((UNITS, rows, K * BLK), f32),
            pltpu.VMEM((RING, UNITS * BLK, features), bf16),
            pltpu.VMEM((2, embed, UNITS * BLK), bf16),
            pltpu.VMEM((2, embed, UNITS * BLK), bf16),
            dma((RING, UNITS)),
            dma((7,)),
            dma((owners,)),
            pltpu.SMEM((most + 1,), i32),
        ],
        compiler_params=pltpu.CompilerParams(vmem_limit_bytes=56 << 20),
        name="pair_terms",
    )(
        all_lines.reshape(trainers, 1, LANES),
        item_features,
        all_users,
        all_lines,
        gin,
        gin_t,
        gout,
        gout_t,
        tower_t,
    )

    block = (height + share, LANES)
    part, user_terms = pl.pallas_call(
        functools.partial(sum_kernel, groups, owners),
        out_shape=(
            jax.ShapeDtypeStruct((groups, height, LANES), bf16),
            jax.ShapeDtypeStruct((share, LANES), f32),
        ),
        in_specs=[hbm],
        out_specs=(vmem, vmem),
        scratch_shapes=[
            pltpu.VMEM((owners, chips) + block, bf16),
            pltpu.VMEM((owners, chips) + block, bf16),
            pltpu.VMEM((owners,) + block, bf16),
            pltpu.VMEM((owners,) + block, bf16),
            pltpu.VMEM((owners - 1,) + block, bf16),
            pltpu.VMEM((owners - 1,) + block, bf16),
            pltpu.VMEM((height, LANES), bf16),
            pltpu.VMEM((groups, height, LANES), bf16),
            dma,
            dma((owners,)),
            dma((owners,)),
            dma((owners,)),
            dma((owners,)),
            dma((owners - 1,)),
            dma((owners - 1,)),
            dma((groups - 1,)),
            dma((groups - 1,)),
        ],
        compiler_params=pltpu.CompilerParams(collective_id=0, has_side_effects=True, vmem_limit_bytes=53 << 20),
        name="sum_terms",
    )(terms)

    return pl.pallas_call(
        functools.partial(finish_kernel, users),
        out_shape=(
            jax.ShapeDtypeStruct((width, embed), f32),
            jax.ShapeDtypeStruct((table, embed), f32),
        ),
        in_specs=[smem, vmem, vmem],
        out_specs=(hbm, hbm),
        scratch_shapes=[
            pltpu.VMEM((width, embed), f32),
            pltpu.VMEM((table, embed), f32),
            dma((2,)),
        ],
        compiler_params=pltpu.CompilerParams(vmem_limit_bytes=8 << 20),
        name="finish",
    )(user_ids, part, user_terms)


def solution(mesh):
    return jax.shard_map(
        shards,
        mesh=mesh,
        in_specs=(
            P("shard", None),
            P(),
            P(),
            P(),
            P(),
            P(),
            P(("blk", "shard"), None),
            P(("blk", "shard")),
            P(("blk", "shard"), None),
            P(("blk", "shard"), None),
            P(("blk", "shard")),
        ),
        out_specs=(P("shard", None), P(("blk", "shard"), None)),
        check_vma=False,
    )
```

```python
import functools
import math

import jax
import jax.numpy as jnp
from jax import lax
from jax.experimental import pallas as pl
from jax.experimental.pallas import tpu as pltpu
from jax.sharding import PartitionSpec as P

K = 8
H = 64
BLK = 128
CAP = 2
LANES = 128
CORES = 2
UNITS = 2
CHUNK = 8
TOWER_PIECES = 2
ACC_PIECES = 4
RING = 4
SCAN_ROWS = 4

NN = (((1,), (0,)), ((), ()))
NT = (((1,), (1,)), ((), ()))
MESH = pl.DeviceIdType.MESH


def dot(left, right, dims=NN):
    return lax.dot_general(left, right, dims, preferred_element_type=jnp.float32)


def gather_kernel(
    groups,
    owners,
    ids_hbm,
    pos_hbm,
    owner_hbm,
    slot_hbm,
    table_hbm,
    gin_hbm,
    gin_b_hbm,
    gout_hbm,
    gout_b_hbm,
    tower_hbm,
    users_out,
    lines_out,
    gin_ref,
    gin_t_ref,
    gout_ref,
    gout_t_ref,
    tower_t_ref,
    users,
    lines,
    ids_ref,
    pos_ref,
    owner_ref,
    slot_ref,
    table_ref,
    gin_in,
    gin_b_in,
    gout_in,
    gout_b_in,
    tower_s,
    load_sem,
    send1,
    recv1,
    send2,
    recv2,
):
    g = lax.axis_index("blk")
    s = lax.axis_index("shard")
    chips = groups // CORES
    core = lax.rem(g, CORES)
    chip = g // CORES
    sister = chip * CORES + (CORES - 1) - core
    partners = [(c, d) for c in range(chips) for d in range(owners) if c or d]
    partners.sort(key=lambda at: -2 * min(at[1], owners - at[1]) - at[0])

    def device(c, d):
        return (lax.rem(chip + c, chips) * CORES + core, lax.rem(s + d, owners))

    barrier = pltpu.get_barrier_semaphore()
    for c, d in partners:
        pl.semaphore_signal(barrier, inc=1, device_id=device(c, d), device_id_type=MESH)
    pl.semaphore_signal(barrier, inc=1, device_id=(sister, s), device_id_type=MESH)
    loads = [
        pltpu.make_async_copy(source, to, load_sem.at[n])
        for n, (source, to) in enumerate(
            (
                (ids_hbm, ids_ref),
                (pos_hbm, pos_ref),
                (owner_hbm, owner_ref),
                (slot_hbm, slot_ref),
                (table_hbm, table_ref),
                (gin_hbm, gin_in),
                (gin_b_hbm, gin_b_in),
                (gout_hbm, gout_in),
                (gout_b_hbm, gout_b_in),
                (tower_hbm, tower_s),
            )
        )
    ]
    for copy in loads:
        copy.start()
    for copy in loads[:5]:
        copy.wait()

    count, picks = pos_ref.shape
    listings = slot_ref.shape[0]
    half = count // 2
    table, embed = table_ref.shape
    rows = half * K
    row = lax.broadcasted_iota(jnp.int32, (rows, table), 0)
    column = lax.broadcasted_iota(jnp.int32, (rows, table), 1)
    block = lax.broadcasted_iota(jnp.int32, (rows, embed), 1) // H
    mine = block == lax.broadcasted_iota(jnp.int32, (rows, embed), 0) % K
    parts = []
    for part in range(2):
        wanted = jnp.zeros((rows, table), jnp.int32)
        for k in range(half):
            wanted = jnp.where(row // K == k, ids_ref[part * half + k], wanted)
        picked = dot(jnp.where(column == wanted, 1.0, 0.0).astype(jnp.bfloat16), table_ref[...])
        picked = jnp.where(mine, picked * (1.0 / math.sqrt(H)), 0.0)
        total = picked[:, :LANES]
        for first in range(LANES, embed, LANES):
            total = total + picked[:, first : first + LANES]
        parts.append(total + pltpu.roll(total, H, 1))
    lane = lax.broadcasted_iota(jnp.int32, (rows, LANES), 1)
    users[core, chip, s] = jnp.where(lane < H, parts[0], parts[1]).astype(jnp.bfloat16)
    lane = lax.broadcasted_iota(jnp.int32, (1, LANES), 1)
    line = jnp.zeros((1, LANES), jnp.int32)
    for k in range(count):
        for p in range(picks):
            line = jnp.where(lane == k * picks + p, pos_ref[k, p], line)
    for j in range(listings):
        line = jnp.where(lane == count * picks + j, owner_ref[0, j], line)
        line = jnp.where(lane == count * picks + listings + j, slot_ref[j], line)
    lines[core, chip, s] = line

    pl.semaphore_wait(barrier, len(partners) + 1)
    copies = []
    for n, (c, d) in enumerate(partners):
        for m, ref in enumerate((users, lines)):
            copy = pltpu.make_async_remote_copy(
                src_ref=ref.at[core, chip, s], dst_ref=ref.at[core, chip, s],
                send_sem=send1.at[m, n], recv_sem=recv1.at[m, n],
                device_id=device(c, d), device_id_type=MESH,
            )
            copy.start()
            copies.append(copy)
    for copy in loads[5:]:
        copy.wait()
    tower_t_ref[...] = tower_s[...].T
    pairs, hidden = gin_in.shape
    to = lax.broadcasted_iota(jnp.int32, (pairs, pairs), 0)
    of = lax.broadcasted_iota(jnp.int32, (pairs, pairs), 1)
    turn = jnp.where(of == (to % K) * K + to // K, 1.0, 0.0).astype(jnp.bfloat16)

    def beside(row, scale):
        column = jnp.broadcast_to(row.astype(jnp.float32), (LANES, row.shape[1])).T[:, :16]
        lane = lax.broadcasted_iota(jnp.int32, column.shape, 1)
        return jnp.where(lane == 0, column * scale, 0.0).astype(jnp.bfloat16)

    gin = dot(turn, gin_in[...])
    gin_ref[...] = gin.astype(jnp.bfloat16)
    gin_t_ref[:, :pairs] = (0.5 * gin.T).astype(jnp.bfloat16)
    gin_t_ref[:, pairs:] = beside(gin_b_in[...], 0.5)
    gout_t = dot(turn, gout_in[...])
    gout_ref[...] = (0.5 * gout_t.T).astype(jnp.bfloat16)
    gout_t_ref[:, :hidden] = gout_t.astype(jnp.bfloat16)
    gout_t_ref[:, hidden:] = dot(turn, beside(gout_b_in[...], 1.0)).astype(jnp.bfloat16)
    for copy in copies:
        copy.wait()
    copies = []
    for m, ref in enumerate((users, lines)):
        copy = pltpu.make_async_remote_copy(
            src_ref=ref.at[core], dst_ref=ref.at[core],
            send_sem=send2.at[m], recv_sem=recv2.at[m],
            device_id=(sister, s), device_id_type=MESH,
        )
        copy.start()
        copies.append(copy)
    for copy in copies:
        copy.wait()
    users_out[...] = users[...]
    lines_out[...] = lines[...]


def pair_kernel(
    groups,
    owners,
    users,
    picks,
    listings,
    lists_ref,
    feat_hbm,
    users_hbm,
    lines_hbm,
    gin_hbm,
    gin_t_hbm,
    gout_hbm,
    gout_t_hbm,
    tower_hbm,
    out_hbm,
    users_ref,
    lines_ref,
    gin_ref,
    gin_t_ref,
    gout_ref,
    gout_t_ref,
    tower_ref,
    out_ref,
    acc,
    uacc,
    logit_s,
    feat_s,
    vec_s,
    grad_s,
    feat_sem,
    load_sem,
    out_sem,
    entries,
):
    g = lax.axis_index("blk")
    s = lax.axis_index("shard")
    chips = groups // CORES
    column_users = groups * users
    half = users // 2
    embed, features = tower_ref.shape
    first_owner = users * picks

    loads = [
        pltpu.make_async_copy(source, to, load_sem.at[n])
        for n, (source, to) in enumerate(
            (
                (tower_hbm, tower_ref),
                (users_hbm, users_ref),
                (lines_hbm, lines_ref),
                (gin_hbm, gin_ref),
                (gin_t_hbm, gin_t_ref),
                (gout_hbm, gout_ref),
                (gout_t_hbm, gout_t_ref),
            )
        )
    ]
    for copy in loads:
        copy.start()

    def scan(turn, n):
        for row in range(SCAN_ROWS):
            for j in range(listings):
                entries[n] = (turn * SCAN_ROWS + row) * listings + j
                mine = lists_ref[turn * SCAN_ROWS + row, 0, first_owner + j] == s
                n = n + mine.astype(jnp.int32)
        return n

    zero = jnp.int32(0)
    listed = lax.fori_loop(0, groups * owners // SCAN_ROWS, scan, zero)
    count = (listed + groups - 1 - g) // groups
    steps = (count + UNITS - 1) // UNITS

    def find(step, unit):
        n = jnp.minimum(step * UNITS + unit, count - 1)
        entry = entries[n * groups + g]
        row = entry // listings
        j = entry - row * listings
        place = row // owners
        group = lax.rem(place, chips) * CORES + place // chips
        slot = lists_ref[row, 0, first_owner + listings + j]
        return slot, lax.rem(row, owners), (group * listings + j) * BLK

    def fetch(step):
        copies = []
        for j in range(UNITS):
            block, _, _ = find(step, j)
            copies.append(
                pltpu.make_async_copy(
                    feat_hbm.at[pl.ds(pl.multiple_of(block * BLK, BLK), BLK)],
                    feat_s.at[lax.rem(step, RING), pl.ds(j * BLK, BLK)],
                    feat_sem.at[lax.rem(step, RING), j],
                )
            )
        return copies

    @pl.when(count > 0)
    def _():
        for copy in fetch(zero):
            copy.start()

    @pl.when(steps > 1)
    def _():
        for copy in fetch(zero + 1):
            copy.start()

    acc[...] = jnp.zeros_like(acc)
    uacc[...] = jnp.zeros_like(uacc)
    grad_s[...] = jnp.zeros_like(grad_s)

    @pl.when(count == 0)
    def _():
        feat_s[0] = jnp.zeros(feat_s.shape[1:], feat_s.dtype)

    for copy in loads:
        copy.wait()
    ones = jnp.ones((16, CHUNK * BLK), jnp.bfloat16)
    order = [
        (r, part * half + k) for part in range(2) for r in range(groups) for k in range(half)
    ]

    def tower_piece(m, step, slot):
        rows = pl.ds(m * (embed // TOWER_PIECES), embed // TOWER_PIECES)
        vectors = dot(tower_ref[rows, :], feat_s[lax.rem(step, RING)], NT)
        vec_s[slot, rows] = vectors.astype(jnp.bfloat16)

    def acc_piece(c, step, slot):
        cut = pl.ds(c * (features // ACC_PIECES), features // ACC_PIECES)
        acc[:, cut] += dot(grad_s[slot], feat_s[lax.rem(step, RING), :, cut])

    def prepare(step, unit):
        _, column, base = find(step, unit)
        slot = lax.rem(step, 2)
        vec = vec_s[slot, :, unit * BLK : (unit + 1) * BLK]
        vec_cat = jnp.concatenate([vec[b * H : (b + 1) * H] for b in range(K)], axis=1)
        near = [(r % CORES, r // CORES, column) for r in range(groups)]
        packed = jnp.concatenate([users_ref[at] for at in near], axis=0)
        vectors = jnp.concatenate([packed[:, :H], packed[:, H:]], axis=0)
        logit_s[unit] = dot(vectors, vec_cat)
        lines = jnp.concatenate([lines_ref[at] for at in near], axis=0)
        place = base + lax.broadcasted_iota(jnp.int32, (groups, BLK), 1)
        targets = []
        for k in range(users):
            hit = lines[:, k * picks : k * picks + 1] == place
            for p in range(k * picks + 1, (k + 1) * picks):
                hit = jnp.logical_or(hit, lines[:, p : p + 1] == place)
            targets.append(jnp.where(hit, 1.0, 0.0))
        return dict(
            unit=unit,
            slot=slot,
            column=column,
            valid=jnp.where(step * UNITS + unit < count, 1.0, 0.0),
            vec_cat=vec_cat,
            vectors=vectors,
            targets=targets,
            rows=[],
        )

    def chunk(state, first):
        unit = state["unit"]
        picked = range(first, first + CHUNK)
        logits = jnp.concatenate(
            [
                jnp.concatenate(
                    [
                        logit_s[unit, u * K : (u + 1) * K, b * BLK : (b + 1) * BLK]
                        for b in range(K)
                    ],
                    axis=0,
                )
                for u in picked
            ],
            axis=1,
        )
        wanted = jnp.concatenate(
            [state["targets"][order[u][1]][order[u][0] : order[u][0] + 1] for u in picked], axis=1
        )
        half_pre = dot(
            gin_t_ref[...], jnp.concatenate([logits.astype(jnp.bfloat16), ones], axis=0)
        )
        yield
        t = jnp.tanh(half_pre)
        up = 1.0 + t
        silu = half_pre * up
        slope = up + silu * (1.0 - t)
        gate = dot(gout_t_ref[...], jnp.concatenate([silu.astype(jnp.bfloat16), ones], axis=0))
        yield
        terms = jnp.exp(gate)
        mixture = terms * (1.0 / jnp.sum(terms, axis=0, keepdims=True))
        scores = jnp.sum(mixture * logits, axis=0, keepdims=True)
        score_grad = (0.5 + 0.5 * jnp.tanh(0.5 * scores) - wanted) * state["valid"]
        weighted = score_grad * mixture
        logit_grad = (weighted * (logits - scores)).astype(jnp.bfloat16)
        back = dot(gout_ref[...], logit_grad)
        yield
        hidden_grad = (back * slope).astype(jnp.bfloat16)
        more = dot(gin_ref[...], hidden_grad)
        yield
        pair = weighted + more
        for n in range(CHUNK):
            state["rows"].append(
                jnp.concatenate(
                    [
                        pair[b * K : (b + 1) * K, n * BLK : (n + 1) * BLK]
                        for b in range(K)
                    ],
                    axis=1,
                )
            )
        if len(state["rows"]) == column_users:
            pair_all = jnp.concatenate(state["rows"], axis=0).astype(jnp.bfloat16)
            uacc[state["column"]] += dot(pair_all, state["vec_cat"], NT)
            vectors_t = state["vectors"].astype(jnp.float32).T.astype(jnp.bfloat16)
            grad = dot(vectors_t, pair_all).astype(jnp.bfloat16)
            grad_s[state["slot"], :, unit * BLK : (unit + 1) * BLK] = jnp.concatenate(
                [grad[:, b * BLK : (b + 1) * BLK] for b in range(K)], axis=0
            )
        yield

    stages = 5

    def step_body(step, carry):
        @pl.when(step + 2 < steps)
        def _():
            for copy in fetch(step + 2):
                copy.start()

        @pl.when(step + 1 < steps)
        def _():
            for copy in fetch(step + 1):
                copy.wait()

        before = jnp.maximum(step - 1, 0)
        after = jnp.minimum(step + 1, steps - 1)
        other = lax.rem(step + 1, 2)
        extras = [functools.partial(tower_piece, m, after, other) for m in range(TOWER_PIECES)]
        extras += [functools.partial(acc_piece, c, before, other) for c in range(ACC_PIECES)]
        states = [prepare(step, unit) for unit in range(UNITS)]
        chunks = [
            chunk(state, first) for state in states for first in range(0, column_users, CHUNK)
        ]
        waves = len(chunks) + stages - 1
        done = 0
        for wave in range(waves):
            for n, work in enumerate(chunks):
                if 0 <= wave - n < stages:
                    next(work)
            while done < len(extras) * (wave + 1) // waves:
                extras[done]()
                done += 1
        return carry

    @pl.when(count > 0)
    def _():
        for copy in fetch(zero):
            copy.wait()
        for m in range(TOWER_PIECES):
            tower_piece(m, zero, 0)
        lax.fori_loop(0, steps, step_body, 0)

    width = features // owners
    height = embed // groups
    share = half * K
    cut = features // ACC_PIECES
    last = jnp.maximum(steps - 1, 0)
    if width < LANES:
        out_ref[...] = jnp.zeros_like(out_ref)
    for d in range(owners):
        for r in range(groups):
            parts = [
                uacc[d, (part * groups + r) * share : (part * groups + r + 1) * share]
                for part in range(2)
            ]
            out_ref[d, r % CORES, r // CORES, height : height + share, :] = (
                jnp.concatenate(parts, axis=1) * (1.0 / math.sqrt(H))
            ).astype(jnp.bfloat16)
    copies = []
    for c in range(ACC_PIECES):
        at = slice(c * cut, (c + 1) * cut)
        block = acc[:, at] + dot(grad_s[lax.rem(last, 2)], feat_s[lax.rem(last, RING), :, at])
        block = block.astype(jnp.bfloat16)
        for d in range(c * cut // width, (c + 1) * cut // width):
            for r in range(groups):
                first = d * width - c * cut
                out_ref[d, r % CORES, r // CORES, 0:height, 0:width] = block[
                    r * height : (r + 1) * height, first : first + width
                ]
            copy = pltpu.make_async_copy(out_ref.at[d], out_hbm.at[d], out_sem.at[d])
            copy.start()
            copies.append(copy)
    for copy in copies:
        copy.wait()


def sum_kernel(
    groups,
    owners,
    in_hbm,
    part_out,
    user_out,
    own,
    recv0,
    both,
    recv1,
    stage,
    recv2,
    part,
    final,
    own_sem,
    send0,
    rsem0,
    send1,
    rsem1,
    send2,
    rsem2,
    send3,
    rsem3,
):
    g = lax.axis_index("blk")
    s = lax.axis_index("shard")
    height = part.shape[0]
    core = lax.rem(g, CORES)
    chip = g // CORES
    sister = chip * CORES + (CORES - 1) - core

    def pick(zero, one):
        return zero * (1 - core) + one * core

    def flip(value, bits):
        to = value
        bit = 1
        while bit <= bits:
            if bits & bit:
                to = to + bit * (1 - 2 * lax.rem(value // bit, 2))
            bit *= 2
        return to

    def mine(n):
        return (
            pick(chip, flip(chip, n & 1)),
            pick(flip(s, n), flip(s, n & ~1)),
            pick(n, n & ~1),
        )

    def other(n):
        return (
            pick(flip(chip, 1), flip(chip, n & 1)),
            pick(flip(s, n), flip(s, n | 1)),
            pick(n, n | 1),
        )

    partner = (pick(flip(chip, 1), chip) * CORES + core, pick(s, flip(s, 1)))
    barrier = pltpu.get_barrier_semaphore()
    for n in range(owners - 1, 0, -1):
        to = (g, flip(s, 1))
        if n > 1:
            at = mine(n)
            to = (at[0] * CORES + core, at[1])
        pl.semaphore_signal(barrier, inc=1, device_id=to, device_id_type=MESH)
    for d in range(1, groups):
        pl.semaphore_signal(
            barrier, inc=1, device_id=(lax.rem(g + d, groups), s), device_id_type=MESH
        )
    local = pltpu.make_async_copy(in_hbm.at[:, core], own, own_sem)
    local.start()
    pl.semaphore_wait(barrier, groups + owners - 2)

    order = list(range(owners - 1, -1, -1))
    first = {}
    for d in order:
        first[d] = pltpu.make_async_remote_copy(
            src_ref=in_hbm.at[flip(s, d), CORES - 1 - core], dst_ref=recv0.at[d],
            send_sem=send0.at[d], recv_sem=rsem0.at[d],
            device_id=(sister, s), device_id_type=MESH,
        )
        first[d].start()
    local.wait()

    def summed(at):
        c, d, n = at
        return own[d, c].astype(jnp.float32) + recv0[n, c].astype(jnp.float32)

    second = {}
    for n in order:
        if n % 2:
            first[n].wait()
            first[n - 1].wait()
        both[n] = summed(other(n)).astype(jnp.bfloat16)
        second[n] = pltpu.make_async_remote_copy(
            src_ref=both.at[n], dst_ref=recv1.at[n],
            send_sem=send1.at[n], recv_sem=rsem1.at[n],
            device_id=partner, device_id_type=MESH,
        )
        second[n].start()
    third = []
    total = None
    for n in order:
        second[n].wait()
        total = summed(mine(n)) + recv1[n].astype(jnp.float32)
        if n:
            stage[n - 1] = total.astype(jnp.bfloat16)
            at = mine(n)
            copy = pltpu.make_async_remote_copy(
                src_ref=stage.at[n - 1], dst_ref=recv2.at[n - 1],
                send_sem=send2.at[n - 1], recv_sem=rsem2.at[n - 1],
                device_id=(at[0] * CORES + core, at[1]), device_id_type=MESH,
            )
            copy.start()
            third.append((n - 1, copy))
    for n, copy in third:
        copy.wait()
        total = total + recv2[n].astype(jnp.float32)
    user_out[...] = total[height:]
    part[...] = total[:height].astype(jnp.bfloat16)

    copies = []
    for d in sorted(range(1, groups), key=lambda d: d % CORES):
        copy = pltpu.make_async_remote_copy(
            src_ref=part, dst_ref=final.at[g],
            send_sem=send3.at[d - 1], recv_sem=rsem3.at[d - 1],
            device_id=(lax.rem(g + d, groups), s), device_id_type=MESH,
        )
        copy.start()
        copies.append(copy)
    final[g] = part[...]
    for copy in copies:
        copy.wait()
    part_out[...] = final[...]


def finish_kernel(
    users, ids_ref, part_ref, user_ref, tower_hbm, user_hbm, tower_out, user_out, sems
):
    groups, height, _ = part_ref.shape
    width = tower_out.shape[0]
    for r in range(groups):
        tower_out[:, r * height : (r + 1) * height] = part_ref[r].astype(jnp.float32).T[:width]
    tower = pltpu.make_async_copy(tower_out, tower_hbm, sems.at[0])
    tower.start()
    half = users // 2
    straight = user_ref[...]
    turned = pltpu.roll(straight, H, 1)
    table, embed = user_out.shape
    row = lax.broadcasted_iota(jnp.int32, (table, LANES), 0)
    low = lax.broadcasted_iota(jnp.int32, (1, LANES), 1) < H
    for first in range(0, embed, LANES):
        total = jnp.zeros((table, LANES), jnp.float32)
        for k in range(users):
            at = (k % half) * K + first // H
            left, right = (straight, turned) if k < half else (turned, straight)
            line = jnp.where(low, left[at : at + 1], right[at + 1 : at + 2])
            total = total + jnp.where(row == ids_ref[k], line, 0.0)
        user_out[:, first : first + LANES] = total
    user = pltpu.make_async_copy(user_out, user_hbm, sems.at[1])
    user.start()
    tower.wait()
    user.wait()


def shards(
    item_features,
    tower_weight,
    gate_in,
    gate_in_bias,
    gate_out,
    gate_out_bias,
    user_table,
    user_ids,
    positive_item,
    listed_owner,
    listed_slot,
):
    groups = lax.axis_size("blk")
    owners = lax.axis_size("shard")
    chips = groups // CORES
    trainers = groups * owners
    listings = listed_slot.shape[0]
    users, picks = positive_item.shape
    table = user_table.shape[0]
    features = item_features.shape[1]
    embed = tower_weight.shape[1]
    hidden = gate_in.shape[1]
    pairs = K * K
    rows = groups * users * K
    share = users // 2 * K
    bf16, f32, i32 = jnp.bfloat16, jnp.float32, jnp.int32
    vmem = pl.BlockSpec(memory_space=pltpu.VMEM)
    smem = pl.BlockSpec(memory_space=pltpu.SMEM)
    hbm = pl.BlockSpec(memory_space=pl.ANY)
    dma = pltpu.SemaphoreType.DMA
    partners = chips * owners - 1

    all_users, all_lines, gin, gin_t, gout, gout_t, tower_t = pl.pallas_call(
        functools.partial(gather_kernel, groups, owners),
        out_shape=(
            jax.ShapeDtypeStruct((CORES, chips, owners, share, LANES), bf16),
            jax.ShapeDtypeStruct((CORES, chips, owners, 1, LANES), i32),
            jax.ShapeDtypeStruct((pairs, hidden), bf16),
            jax.ShapeDtypeStruct((hidden, pairs + 16), bf16),
            jax.ShapeDtypeStruct((hidden, pairs), bf16),
            jax.ShapeDtypeStruct((pairs, hidden + 16), bf16),
            jax.ShapeDtypeStruct((embed, features), bf16),
        ),
        in_specs=[hbm] * 10,
        out_specs=(vmem,) * 7,
        scratch_shapes=[
            pltpu.VMEM((CORES, chips, owners, share, LANES), bf16),
            pltpu.VMEM((CORES, chips, owners, 1, LANES), i32),
            pltpu.SMEM((users,), i32),
            pltpu.SMEM((users, picks), i32),
            pltpu.SMEM((1, listings), i32),
            pltpu.SMEM((listings,), i32),
            pltpu.VMEM((table, embed), bf16),
            pltpu.VMEM((pairs, hidden), bf16),
            pltpu.VMEM((1, hidden), bf16),
            pltpu.VMEM((pairs, hidden), bf16),
            pltpu.VMEM((1, pairs), bf16),
            pltpu.VMEM((features, embed), bf16),
            dma((10,)),
            dma((2, partners)),
            dma((2, partners)),
            dma((2,)),
            dma((2,)),
        ],
        compiler_params=pltpu.CompilerParams(collective_id=1, has_side_effects=True),
        name="gather_users",
    )(
        user_ids,
        positive_item,
        listed_owner.T,
        listed_slot,
        user_table,
        gate_in,
        gate_in_bias[None, :],
        gate_out.T,
        gate_out_bias[None, :],
        tower_weight,
    )

    most = trainers * min(CAP, listings)
    height = embed // groups
    width = features // owners
    terms = pl.pallas_call(
        functools.partial(pair_kernel, groups, owners, users, picks, listings),
        out_shape=jax.ShapeDtypeStruct((owners, CORES, chips, height + share, LANES), bf16),
        in_specs=[smem] + [hbm] * 8,
        out_specs=hbm,
        scratch_shapes=[
            pltpu.VMEM((CORES, chips, owners, share, LANES), bf16),
            pltpu.VMEM((CORES, chips, owners, 1, LANES), i32),
            pltpu.VMEM((pairs, hidden), bf16),
            pltpu.VMEM((hidden, pairs + 16), bf16),
            pltpu.VMEM((hidden, pairs), bf16),
            pltpu.VMEM((pairs, hidden + 16), bf16),
            pltpu.VMEM((embed, features), bf16),
            pltpu.VMEM((owners, CORES, chips, height + share, LANES), bf16),
            pltpu.VMEM((embed, features), f32),
            pltpu.VMEM((owners, rows, H), f32),
            pltpu.VMEM((UNITS, rows, K * BLK), f32),
            pltpu.VMEM((RING, UNITS * BLK, features), bf16),
            pltpu.VMEM((2, embed, UNITS * BLK), bf16),
            pltpu.VMEM((2, embed, UNITS * BLK), bf16),
            dma((RING, UNITS)),
            dma((7,)),
            dma((owners,)),
            pltpu.SMEM((most + 1,), i32),
        ],
        compiler_params=pltpu.CompilerParams(vmem_limit_bytes=56 << 20),
        name="pair_terms",
    )(
        all_lines.reshape(trainers, 1, LANES),
        item_features,
        all_users,
        all_lines,
        gin,
        gin_t,
        gout,
        gout_t,
        tower_t,
    )

    block = (height + share, LANES)
    part, user_terms = pl.pallas_call(
        functools.partial(sum_kernel, groups, owners),
        out_shape=(
            jax.ShapeDtypeStruct((groups, height, LANES), bf16),
            jax.ShapeDtypeStruct((share, LANES), f32),
        ),
        in_specs=[hbm],
        out_specs=(vmem, vmem),
        scratch_shapes=[
            pltpu.VMEM((owners, chips) + block, bf16),
            pltpu.VMEM((owners, chips) + block, bf16),
            pltpu.VMEM((owners,) + block, bf16),
            pltpu.VMEM((owners,) + block, bf16),
            pltpu.VMEM((owners - 1,) + block, bf16),
            pltpu.VMEM((owners - 1,) + block, bf16),
            pltpu.VMEM((height, LANES), bf16),
            pltpu.VMEM((groups, height, LANES), bf16),
            dma,
            dma((owners,)),
            dma((owners,)),
            dma((owners,)),
            dma((owners,)),
            dma((owners - 1,)),
            dma((owners - 1,)),
            dma((groups - 1,)),
            dma((groups - 1,)),
        ],
        compiler_params=pltpu.CompilerParams(collective_id=0, has_side_effects=True, vmem_limit_bytes=53 << 20),
        name="sum_terms",
    )(terms)

    return pl.pallas_call(
        functools.partial(finish_kernel, users),
        out_shape=(
            jax.ShapeDtypeStruct((width, embed), f32),
            jax.ShapeDtypeStruct((table, embed), f32),
        ),
        in_specs=[smem, vmem, vmem],
        out_specs=(hbm, hbm),
        scratch_shapes=[
            pltpu.VMEM((width, embed), f32),
            pltpu.VMEM((table, embed), f32),
            dma((2,)),
        ],
        compiler_params=pltpu.CompilerParams(vmem_limit_bytes=8 << 20),
        name="finish",
    )(user_ids, part, user_terms)


def solution(mesh):
    return jax.shard_map(
        shards,
        mesh=mesh,
        in_specs=(
            P("shard", None),
            P(),
            P(),
            P(),
            P(),
            P(),
            P(("blk", "shard"), None),
            P(("blk", "shard")),
            P(("blk", "shard"), None),
            P(("blk", "shard"), None),
            P(("blk", "shard")),
        ),
        out_specs=(P("shard", None), P(("blk", "shard"), None)),
        check_vma=False,
    )
```

```python
import functools
import math

import jax
import jax.numpy as jnp
from jax import lax
from jax.experimental import pallas as pl
from jax.experimental.pallas import tpu as pltpu
from jax.sharding import PartitionSpec as P

K = 8
H = 64
BLK = 128
CAP = 2
LANES = 128
CORES = 2
UNITS = 2
CHUNK = 8
TOWER_PIECES = 2
ACC_PIECES = 4
RING = 4
SCAN_ROWS = 4

NN = (((1,), (0,)), ((), ()))
NT = (((1,), (1,)), ((), ()))
MESH = pl.DeviceIdType.MESH


def dot(left, right, dims=NN):
    return lax.dot_general(left, right, dims, preferred_element_type=jnp.float32)


def gather_kernel(
    groups,
    owners,
    ids_hbm,
    pos_hbm,
    owner_hbm,
    slot_hbm,
    table_hbm,
    gin_hbm,
    gin_b_hbm,
    gout_hbm,
    gout_b_hbm,
    tower_hbm,
    users_out,
    lines_out,
    gin_out,
    gin_t_out,
    gout_out,
    gout_t_out,
    tower_t_out,
    gin_ref,
    gin_t_ref,
    gout_ref,
    gout_t_ref,
    tower_t_ref,
    users,
    lines,
    ids_ref,
    pos_ref,
    owner_ref,
    slot_ref,
    table_ref,
    gin_in,
    gin_b_in,
    gout_in,
    gout_b_in,
    tower_s,
    load_sem,
    store_sem,
    send1,
    recv1,
    send2,
    recv2,
):
    g = lax.axis_index("blk")
    s = lax.axis_index("shard")
    chips = groups // CORES
    core = lax.rem(g, CORES)
    chip = g // CORES
    sister = chip * CORES + (CORES - 1) - core
    partners = [(c, d) for c in range(chips) for d in range(owners) if c or d]
    partners.sort(key=lambda at: -2 * min(at[1], owners - at[1]) - at[0])

    def device(c, d):
        return (lax.rem(chip + c, chips) * CORES + core, lax.rem(s + d, owners))

    barrier = pltpu.get_barrier_semaphore()
    for c, d in partners:
        pl.semaphore_signal(barrier, inc=1, device_id=device(c, d), device_id_type=MESH)
    pl.semaphore_signal(barrier, inc=1, device_id=(sister, s), device_id_type=MESH)
    loads = [
        pltpu.make_async_copy(source, to, load_sem.at[n])
        for n, (source, to) in enumerate(
            (
                (ids_hbm, ids_ref),
                (pos_hbm, pos_ref),
                (owner_hbm, owner_ref),
                (slot_hbm, slot_ref),
                (table_hbm, table_ref),
                (gin_hbm, gin_in),
                (gin_b_hbm, gin_b_in),
                (gout_hbm, gout_in),
                (gout_b_hbm, gout_b_in),
                (tower_hbm, tower_s),
            )
        )
    ]
    for copy in loads:
        copy.start()
    for copy in loads[:5]:
        copy.wait()

    count, picks = pos_ref.shape
    listings = slot_ref.shape[0]
    half = count // 2
    table, embed = table_ref.shape
    rows = half * K
    row = lax.broadcasted_iota(jnp.int32, (rows, table), 0)
    column = lax.broadcasted_iota(jnp.int32, (rows, table), 1)
    block = lax.broadcasted_iota(jnp.int32, (rows, embed), 1) // H
    mine = block == lax.broadcasted_iota(jnp.int32, (rows, embed), 0) % K
    parts = []
    for part in range(2):
        wanted = jnp.zeros((rows, table), jnp.int32)
        for k in range(half):
            wanted = jnp.where(row // K == k, ids_ref[part * half + k], wanted)
        picked = dot(jnp.where(column == wanted, 1.0, 0.0).astype(jnp.bfloat16), table_ref[...])
        picked = jnp.where(mine, picked * (1.0 / math.sqrt(H)), 0.0)
        total = picked[:, :LANES]
        for first in range(LANES, embed, LANES):
            total = total + picked[:, first : first + LANES]
        parts.append(total + pltpu.roll(total, H, 1))
    lane = lax.broadcasted_iota(jnp.int32, (rows, LANES), 1)
    users[core, chip, s] = jnp.where(lane < H, parts[0], parts[1]).astype(jnp.bfloat16)
    lane = lax.broadcasted_iota(jnp.int32, (1, LANES), 1)
    line = jnp.zeros((1, LANES), jnp.int32)
    for k in range(count):
        for p in range(picks):
            line = jnp.where(lane == k * picks + p, pos_ref[k, p], line)
    for j in range(listings):
        line = jnp.where(lane == count * picks + j, owner_ref[0, j], line)
        line = jnp.where(lane == count * picks + listings + j, slot_ref[j], line)
    lines[core, chip, s] = line

    pl.semaphore_wait(barrier, len(partners) + 1)
    copies = []
    for n, (c, d) in enumerate(partners):
        for m, ref in enumerate((users, lines)):
            copy = pltpu.make_async_remote_copy(
                src_ref=ref.at[core, chip, s], dst_ref=ref.at[core, chip, s],
                send_sem=send1.at[m, n], recv_sem=recv1.at[m, n],
                device_id=device(c, d), device_id_type=MESH,
            )
            copy.start()
            copies.append(copy)
    for copy in loads[5:]:
        copy.wait()
    tower_t_ref[...] = tower_s[...].T
    pairs, hidden = gin_in.shape
    to = lax.broadcasted_iota(jnp.int32, (pairs, pairs), 0)
    of = lax.broadcasted_iota(jnp.int32, (pairs, pairs), 1)
    turn = jnp.where(of == (to % K) * K + to // K, 1.0, 0.0).astype(jnp.bfloat16)

    def beside(row, scale):
        column = jnp.broadcast_to(row.astype(jnp.float32), (LANES, row.shape[1])).T[:, :16]
        lane = lax.broadcasted_iota(jnp.int32, column.shape, 1)
        return jnp.where(lane == 0, column * scale, 0.0).astype(jnp.bfloat16)

    gin = dot(turn, gin_in[...])
    gin_ref[...] = gin.astype(jnp.bfloat16)
    gin_t_ref[:, :pairs] = (0.5 * gin.T).astype(jnp.bfloat16)
    gin_t_ref[:, pairs:] = beside(gin_b_in[...], 0.5)
    gout_t = dot(turn, gout_in[...])
    gout_ref[...] = (0.5 * gout_t.T).astype(jnp.bfloat16)
    gout_t_ref[:, :hidden] = gout_t.astype(jnp.bfloat16)
    gout_t_ref[:, hidden:] = dot(turn, beside(gout_b_in[...], 1.0)).astype(jnp.bfloat16)
    stores = [
        pltpu.make_async_copy(source, to, store_sem.at[n])
        for n, (source, to) in enumerate(
            (
                (tower_t_ref, tower_t_out),
                (gin_ref, gin_out),
                (gin_t_ref, gin_t_out),
                (gout_ref, gout_out),
                (gout_t_ref, gout_t_out),
                (users, users_out),
                (lines, lines_out),
            )
        )
    ]
    for copy in stores[:5]:
        copy.start()
    for copy in copies:
        copy.wait()
    copies = []
    for m, ref in enumerate((users, lines)):
        copy = pltpu.make_async_remote_copy(
            src_ref=ref.at[core], dst_ref=ref.at[core],
            send_sem=send2.at[m], recv_sem=recv2.at[m],
            device_id=(sister, s), device_id_type=MESH,
        )
        copy.start()
        copies.append(copy)
    for copy in copies:
        copy.wait()
    for copy in stores[5:]:
        copy.start()
    for copy in stores:
        copy.wait()


def pair_kernel(
    groups,
    owners,
    users,
    picks,
    listings,
    lists_ref,
    feat_hbm,
    users_hbm,
    lines_hbm,
    gin_hbm,
    gin_t_hbm,
    gout_hbm,
    gout_t_hbm,
    tower_hbm,
    out_hbm,
    users_ref,
    lines_ref,
    gin_ref,
    gin_t_ref,
    gout_ref,
    gout_t_ref,
    tower_ref,
    out_ref,
    acc,
    uacc,
    logit_s,
    feat_s,
    vec_s,
    grad_s,
    feat_sem,
    load_sem,
    out_sem,
    entries,
):
    g = lax.axis_index("blk")
    s = lax.axis_index("shard")
    chips = groups // CORES
    column_users = groups * users
    half = users // 2
    embed, features = tower_ref.shape
    first_owner = users * picks

    loads = [
        pltpu.make_async_copy(source, to, load_sem.at[n])
        for n, (source, to) in enumerate(
            (
                (tower_hbm, tower_ref),
                (users_hbm, users_ref),
                (lines_hbm, lines_ref),
                (gin_hbm, gin_ref),
                (gin_t_hbm, gin_t_ref),
                (gout_hbm, gout_ref),
                (gout_t_hbm, gout_t_ref),
            )
        )
    ]
    for copy in loads:
        copy.start()

    def scan(turn, n):
        for row in range(SCAN_ROWS):
            for j in range(listings):
                entries[n] = (turn * SCAN_ROWS + row) * listings + j
                mine = lists_ref[turn * SCAN_ROWS + row, 0, first_owner + j] == s
                n = n + mine.astype(jnp.int32)
        return n

    zero = jnp.int32(0)
    listed = lax.fori_loop(0, groups * owners // SCAN_ROWS, scan, zero)
    count = (listed + groups - 1 - g) // groups
    steps = (count + UNITS - 1) // UNITS

    def find(step, unit):
        n = jnp.minimum(step * UNITS + unit, count - 1)
        entry = entries[n * groups + g]
        row = entry // listings
        j = entry - row * listings
        place = row // owners
        group = lax.rem(place, chips) * CORES + place // chips
        slot = lists_ref[row, 0, first_owner + listings + j]
        return slot, lax.rem(row, owners), (group * listings + j) * BLK

    def fetch(step):
        copies = []
        for j in range(UNITS):
            block, _, _ = find(step, j)
            copies.append(
                pltpu.make_async_copy(
                    feat_hbm.at[pl.ds(pl.multiple_of(block * BLK, BLK), BLK)],
                    feat_s.at[lax.rem(step, RING), pl.ds(j * BLK, BLK)],
                    feat_sem.at[lax.rem(step, RING), j],
                )
            )
        return copies

    @pl.when(count > 0)
    def _():
        for copy in fetch(zero):
            copy.start()

    @pl.when(steps > 1)
    def _():
        for copy in fetch(zero + 1):
            copy.start()

    acc[...] = jnp.zeros_like(acc)
    uacc[...] = jnp.zeros_like(uacc)
    grad_s[...] = jnp.zeros_like(grad_s)

    @pl.when(count == 0)
    def _():
        feat_s[0] = jnp.zeros(feat_s.shape[1:], feat_s.dtype)

    for copy in loads:
        copy.wait()
    ones = jnp.ones((16, CHUNK * BLK), jnp.bfloat16)
    order = [
        (r, part * half + k) for part in range(2) for r in range(groups) for k in range(half)
    ]

    def tower_piece(m, step, slot):
        rows = pl.ds(m * (embed // TOWER_PIECES), embed // TOWER_PIECES)
        vectors = dot(tower_ref[rows, :], feat_s[lax.rem(step, RING)], NT)
        vec_s[slot, rows] = vectors.astype(jnp.bfloat16)

    def acc_piece(c, step, slot):
        cut = pl.ds(c * (features // ACC_PIECES), features // ACC_PIECES)
        acc[:, cut] += dot(grad_s[slot], feat_s[lax.rem(step, RING), :, cut])

    def prepare(step, unit):
        _, column, base = find(step, unit)
        slot = lax.rem(step, 2)
        vec = vec_s[slot, :, unit * BLK : (unit + 1) * BLK]
        vec_cat = jnp.concatenate([vec[b * H : (b + 1) * H] for b in range(K)], axis=1)
        near = [(r % CORES, r // CORES, column) for r in range(groups)]
        packed = jnp.concatenate([users_ref[at] for at in near], axis=0)
        vectors = jnp.concatenate([packed[:, :H], packed[:, H:]], axis=0)
        logit_s[unit] = dot(vectors, vec_cat)
        lines = jnp.concatenate([lines_ref[at] for at in near], axis=0)
        place = base + lax.broadcasted_iota(jnp.int32, (groups, BLK), 1)
        targets = []
        for k in range(users):
            hit = lines[:, k * picks : k * picks + 1] == place
            for p in range(k * picks + 1, (k + 1) * picks):
                hit = jnp.logical_or(hit, lines[:, p : p + 1] == place)
            targets.append(jnp.where(hit, 1.0, 0.0))
        return dict(
            unit=unit,
            slot=slot,
            column=column,
            valid=jnp.where(step * UNITS + unit < count, 1.0, 0.0),
            vec_cat=vec_cat,
            vectors=vectors,
            targets=targets,
            rows=[],
        )

    def chunk(state, first):
        unit = state["unit"]
        picked = range(first, first + CHUNK)
        logits = jnp.concatenate(
            [
                jnp.concatenate(
                    [
                        logit_s[unit, u * K : (u + 1) * K, b * BLK : (b + 1) * BLK]
                        for b in range(K)
                    ],
                    axis=0,
                )
                for u in picked
            ],
            axis=1,
        )
        wanted = jnp.concatenate(
            [state["targets"][order[u][1]][order[u][0] : order[u][0] + 1] for u in picked], axis=1
        )
        half_pre = dot(
            gin_t_ref[...], jnp.concatenate([logits.astype(jnp.bfloat16), ones], axis=0)
        )
        yield
        t = jnp.tanh(half_pre)
        up = 1.0 + t
        silu = half_pre * up
        slope = up + silu * (1.0 - t)
        gate = dot(gout_t_ref[...], jnp.concatenate([silu.astype(jnp.bfloat16), ones], axis=0))
        yield
        terms = jnp.exp(gate)
        mixture = terms * (1.0 / jnp.sum(terms, axis=0, keepdims=True))
        scores = jnp.sum(mixture * logits, axis=0, keepdims=True)
        score_grad = (0.5 + 0.5 * jnp.tanh(0.5 * scores) - wanted) * state["valid"]
        weighted = score_grad * mixture
        logit_grad = (weighted * (logits - scores)).astype(jnp.bfloat16)
        back = dot(gout_ref[...], logit_grad)
        yield
        hidden_grad = (back * slope).astype(jnp.bfloat16)
        more = dot(gin_ref[...], hidden_grad)
        yield
        pair = weighted + more
        for n in range(CHUNK):
            state["rows"].append(
                jnp.concatenate(
                    [
                        pair[b * K : (b + 1) * K, n * BLK : (n + 1) * BLK]
                        for b in range(K)
                    ],
                    axis=1,
                )
            )
        if len(state["rows"]) == column_users:
            pair_all = jnp.concatenate(state["rows"], axis=0).astype(jnp.bfloat16)
            uacc[state["column"]] += dot(pair_all, state["vec_cat"], NT)
            vectors_t = state["vectors"].astype(jnp.float32).T.astype(jnp.bfloat16)
            grad = dot(vectors_t, pair_all).astype(jnp.bfloat16)
            grad_s[state["slot"], :, unit * BLK : (unit + 1) * BLK] = jnp.concatenate(
                [grad[:, b * BLK : (b + 1) * BLK] for b in range(K)], axis=0
            )
        yield

    stages = 5

    def step_body(step, carry):
        @pl.when(step + 2 < steps)
        def _():
            for copy in fetch(step + 2):
                copy.start()

        @pl.when(step + 1 < steps)
        def _():
            for copy in fetch(step + 1):
                copy.wait()

        before = jnp.maximum(step - 1, 0)
        after = jnp.minimum(step + 1, steps - 1)
        other = lax.rem(step + 1, 2)
        extras = [functools.partial(tower_piece, m, after, other) for m in range(TOWER_PIECES)]
        extras += [functools.partial(acc_piece, c, before, other) for c in range(ACC_PIECES)]
        states = [prepare(step, unit) for unit in range(UNITS)]
        chunks = [
            chunk(state, first) for state in states for first in range(0, column_users, CHUNK)
        ]
        waves = len(chunks) + stages - 1
        done = 0
        for wave in range(waves):
            for n, work in enumerate(chunks):
                if 0 <= wave - n < stages:
                    next(work)
            while done < len(extras) * (wave + 1) // waves:
                extras[done]()
                done += 1
        return carry

    @pl.when(count > 0)
    def _():
        for copy in fetch(zero):
            copy.wait()
        for m in range(TOWER_PIECES):
            tower_piece(m, zero, 0)
        lax.fori_loop(0, steps, step_body, 0)

    width = features // owners
    height = embed // groups
    share = half * K
    cut = features // ACC_PIECES
    last = jnp.maximum(steps - 1, 0)
    if width < LANES:
        out_ref[...] = jnp.zeros_like(out_ref)
    for d in range(owners):
        for r in range(groups):
            parts = [
                uacc[d, (part * groups + r) * share : (part * groups + r + 1) * share]
                for part in range(2)
            ]
            out_ref[d, r % CORES, r // CORES, height : height + share, :] = (
                jnp.concatenate(parts, axis=1) * (1.0 / math.sqrt(H))
            ).astype(jnp.bfloat16)
    copies = []
    for c in range(ACC_PIECES):
        at = slice(c * cut, (c + 1) * cut)
        block = acc[:, at] + dot(grad_s[lax.rem(last, 2)], feat_s[lax.rem(last, RING), :, at])
        block = block.astype(jnp.bfloat16)
        for d in range(c * cut // width, (c + 1) * cut // width):
            for r in range(groups):
                first = d * width - c * cut
                out_ref[d, r % CORES, r // CORES, 0:height, 0:width] = block[
                    r * height : (r + 1) * height, first : first + width
                ]
            copy = pltpu.make_async_copy(out_ref.at[d], out_hbm.at[d], out_sem.at[d])
            copy.start()
            copies.append(copy)
    for copy in copies:
        copy.wait()


def sum_kernel(
    groups,
    owners,
    in_hbm,
    part_out,
    user_out,
    own,
    recv0,
    both,
    recv1,
    stage,
    recv2,
    part,
    final,
    own_sem,
    send0,
    rsem0,
    send1,
    rsem1,
    send2,
    rsem2,
    send3,
    rsem3,
):
    g = lax.axis_index("blk")
    s = lax.axis_index("shard")
    height = part.shape[0]
    core = lax.rem(g, CORES)
    chip = g // CORES
    sister = chip * CORES + (CORES - 1) - core

    def pick(zero, one):
        return zero * (1 - core) + one * core

    def flip(value, bits):
        to = value
        bit = 1
        while bit <= bits:
            if bits & bit:
                to = to + bit * (1 - 2 * lax.rem(value // bit, 2))
            bit *= 2
        return to

    def mine(n):
        return (
            pick(chip, flip(chip, n & 1)),
            pick(flip(s, n), flip(s, n & ~1)),
            pick(n, n & ~1),
        )

    def other(n):
        return (
            pick(flip(chip, 1), flip(chip, n & 1)),
            pick(flip(s, n), flip(s, n | 1)),
            pick(n, n | 1),
        )

    partner = (pick(flip(chip, 1), chip) * CORES + core, pick(s, flip(s, 1)))
    barrier = pltpu.get_barrier_semaphore()
    for n in range(owners - 1, 0, -1):
        to = (g, flip(s, 1))
        if n > 1:
            at = mine(n)
            to = (at[0] * CORES + core, at[1])
        pl.semaphore_signal(barrier, inc=1, device_id=to, device_id_type=MESH)
    for d in range(1, groups):
        pl.semaphore_signal(
            barrier, inc=1, device_id=(lax.rem(g + d, groups), s), device_id_type=MESH
        )
    local = pltpu.make_async_copy(in_hbm.at[:, core], own, own_sem)
    local.start()
    pl.semaphore_wait(barrier, groups + owners - 2)

    order = list(range(owners - 1, -1, -1))
    first = {}
    for d in order:
        first[d] = pltpu.make_async_remote_copy(
            src_ref=in_hbm.at[flip(s, d), CORES - 1 - core], dst_ref=recv0.at[d],
            send_sem=send0.at[d], recv_sem=rsem0.at[d],
            device_id=(sister, s), device_id_type=MESH,
        )
        first[d].start()
    local.wait()

    def summed(at):
        c, d, n = at
        return own[d, c].astype(jnp.float32) + recv0[n, c].astype(jnp.float32)

    second = {}
    for n in order:
        if n % 2:
            first[n].wait()
            first[n - 1].wait()
        both[n] = summed(other(n)).astype(jnp.bfloat16)
        second[n] = pltpu.make_async_remote_copy(
            src_ref=both.at[n], dst_ref=recv1.at[n],
            send_sem=send1.at[n], recv_sem=rsem1.at[n],
            device_id=partner, device_id_type=MESH,
        )
        second[n].start()
    third = []
    total = None
    for n in order:
        second[n].wait()
        total = summed(mine(n)) + recv1[n].astype(jnp.float32)
        if n:
            stage[n - 1] = total.astype(jnp.bfloat16)
            at = mine(n)
            copy = pltpu.make_async_remote_copy(
                src_ref=stage.at[n - 1], dst_ref=recv2.at[n - 1],
                send_sem=send2.at[n - 1], recv_sem=rsem2.at[n - 1],
                device_id=(at[0] * CORES + core, at[1]), device_id_type=MESH,
            )
            copy.start()
            third.append((n - 1, copy))
    for n, copy in third:
        copy.wait()
        total = total + recv2[n].astype(jnp.float32)
    user_out[...] = total[height:]
    part[...] = total[:height].astype(jnp.bfloat16)

    copies = []
    for d in sorted(range(1, groups), key=lambda d: d % CORES):
        copy = pltpu.make_async_remote_copy(
            src_ref=part, dst_ref=final.at[g],
            send_sem=send3.at[d - 1], recv_sem=rsem3.at[d - 1],
            device_id=(lax.rem(g + d, groups), s), device_id_type=MESH,
        )
        copy.start()
        copies.append(copy)
    final[g] = part[...]
    for copy in copies:
        copy.wait()
    part_out[...] = final[...]


def finish_kernel(
    users, ids_ref, part_ref, user_ref, tower_hbm, user_hbm, tower_out, user_out, sems
):
    groups, height, _ = part_ref.shape
    width = tower_out.shape[0]
    for r in range(groups):
        tower_out[:, r * height : (r + 1) * height] = part_ref[r].astype(jnp.float32).T[:width]
    tower = pltpu.make_async_copy(tower_out, tower_hbm, sems.at[0])
    tower.start()
    half = users // 2
    straight = user_ref[...]
    turned = pltpu.roll(straight, H, 1)
    table, embed = user_out.shape
    row = lax.broadcasted_iota(jnp.int32, (table, LANES), 0)
    low = lax.broadcasted_iota(jnp.int32, (1, LANES), 1) < H
    for first in range(0, embed, LANES):
        total = jnp.zeros((table, LANES), jnp.float32)
        for k in range(users):
            at = (k % half) * K + first // H
            left, right = (straight, turned) if k < half else (turned, straight)
            line = jnp.where(low, left[at : at + 1], right[at + 1 : at + 2])
            total = total + jnp.where(row == ids_ref[k], line, 0.0)
        user_out[:, first : first + LANES] = total
    user = pltpu.make_async_copy(user_out, user_hbm, sems.at[1])
    user.start()
    tower.wait()
    user.wait()


def shards(
    item_features,
    tower_weight,
    gate_in,
    gate_in_bias,
    gate_out,
    gate_out_bias,
    user_table,
    user_ids,
    positive_item,
    listed_owner,
    listed_slot,
):
    groups = lax.axis_size("blk")
    owners = lax.axis_size("shard")
    chips = groups // CORES
    trainers = groups * owners
    listings = listed_slot.shape[0]
    users, picks = positive_item.shape
    table = user_table.shape[0]
    features = item_features.shape[1]
    embed = tower_weight.shape[1]
    hidden = gate_in.shape[1]
    pairs = K * K
    rows = groups * users * K
    share = users // 2 * K
    bf16, f32, i32 = jnp.bfloat16, jnp.float32, jnp.int32
    vmem = pl.BlockSpec(memory_space=pltpu.VMEM)
    smem = pl.BlockSpec(memory_space=pltpu.SMEM)
    hbm = pl.BlockSpec(memory_space=pl.ANY)
    dma = pltpu.SemaphoreType.DMA
    partners = chips * owners - 1

    all_users, all_lines, gin, gin_t, gout, gout_t, tower_t = pl.pallas_call(
        functools.partial(gather_kernel, groups, owners),
        out_shape=(
            jax.ShapeDtypeStruct((CORES, chips, owners, share, LANES), bf16),
            jax.ShapeDtypeStruct((CORES, chips, owners, 1, LANES), i32),
            jax.ShapeDtypeStruct((pairs, hidden), bf16),
            jax.ShapeDtypeStruct((hidden, pairs + 16), bf16),
            jax.ShapeDtypeStruct((hidden, pairs), bf16),
            jax.ShapeDtypeStruct((pairs, hidden + 16), bf16),
            jax.ShapeDtypeStruct((embed, features), bf16),
        ),
        in_specs=[hbm] * 10,
        out_specs=(hbm,) * 7,
        scratch_shapes=[
            pltpu.VMEM((pairs, hidden), bf16),
            pltpu.VMEM((hidden, pairs + 16), bf16),
            pltpu.VMEM((hidden, pairs), bf16),
            pltpu.VMEM((pairs, hidden + 16), bf16),
            pltpu.VMEM((embed, features), bf16),
            pltpu.VMEM((CORES, chips, owners, share, LANES), bf16),
            pltpu.VMEM((CORES, chips, owners, 1, LANES), i32),
            pltpu.SMEM((users,), i32),
            pltpu.SMEM((users, picks), i32),
            pltpu.SMEM((1, listings), i32),
            pltpu.SMEM((listings,), i32),
            pltpu.VMEM((table, embed), bf16),
            pltpu.VMEM((pairs, hidden), bf16),
            pltpu.VMEM((1, hidden), bf16),
            pltpu.VMEM((pairs, hidden), bf16),
            pltpu.VMEM((1, pairs), bf16),
            pltpu.VMEM((features, embed), bf16),
            dma((10,)),
            dma((7,)),
            dma((2, partners)),
            dma((2, partners)),
            dma((2,)),
            dma((2,)),
        ],
        compiler_params=pltpu.CompilerParams(collective_id=1, has_side_effects=True),
        name="gather_users",
    )(
        user_ids,
        positive_item,
        listed_owner.T,
        listed_slot,
        user_table,
        gate_in,
        gate_in_bias[None, :],
        gate_out.T,
        gate_out_bias[None, :],
        tower_weight,
    )

    most = trainers * min(CAP, listings)
    height = embed // groups
    width = features // owners
    terms = pl.pallas_call(
        functools.partial(pair_kernel, groups, owners, users, picks, listings),
        out_shape=jax.ShapeDtypeStruct((owners, CORES, chips, height + share, LANES), bf16),
        in_specs=[smem] + [hbm] * 8,
        out_specs=hbm,
        scratch_shapes=[
            pltpu.VMEM((CORES, chips, owners, share, LANES), bf16),
            pltpu.VMEM((CORES, chips, owners, 1, LANES), i32),
            pltpu.VMEM((pairs, hidden), bf16),
            pltpu.VMEM((hidden, pairs + 16), bf16),
            pltpu.VMEM((hidden, pairs), bf16),
            pltpu.VMEM((pairs, hidden + 16), bf16),
            pltpu.VMEM((embed, features), bf16),
            pltpu.VMEM((owners, CORES, chips, height + share, LANES), bf16),
            pltpu.VMEM((embed, features), f32),
            pltpu.VMEM((owners, rows, H), f32),
            pltpu.VMEM((UNITS, rows, K * BLK), f32),
            pltpu.VMEM((RING, UNITS * BLK, features), bf16),
            pltpu.VMEM((2, embed, UNITS * BLK), bf16),
            pltpu.VMEM((2, embed, UNITS * BLK), bf16),
            dma((RING, UNITS)),
            dma((7,)),
            dma((owners,)),
            pltpu.SMEM((most + 1,), i32),
        ],
        compiler_params=pltpu.CompilerParams(vmem_limit_bytes=56 << 20),
        name="pair_terms",
    )(
        all_lines.reshape(trainers, 1, LANES),
        item_features,
        all_users,
        all_lines,
        gin,
        gin_t,
        gout,
        gout_t,
        tower_t,
    )

    block = (height + share, LANES)
    part, user_terms = pl.pallas_call(
        functools.partial(sum_kernel, groups, owners),
        out_shape=(
            jax.ShapeDtypeStruct((groups, height, LANES), bf16),
            jax.ShapeDtypeStruct((share, LANES), f32),
        ),
        in_specs=[hbm],
        out_specs=(vmem, vmem),
        scratch_shapes=[
            pltpu.VMEM((owners, chips) + block, bf16),
            pltpu.VMEM((owners, chips) + block, bf16),
            pltpu.VMEM((owners,) + block, bf16),
            pltpu.VMEM((owners,) + block, bf16),
            pltpu.VMEM((owners - 1,) + block, bf16),
            pltpu.VMEM((owners - 1,) + block, bf16),
            pltpu.VMEM((height, LANES), bf16),
            pltpu.VMEM((groups, height, LANES), bf16),
            dma,
            dma((owners,)),
            dma((owners,)),
            dma((owners,)),
            dma((owners,)),
            dma((owners - 1,)),
            dma((owners - 1,)),
            dma((groups - 1,)),
            dma((groups - 1,)),
        ],
        compiler_params=pltpu.CompilerParams(collective_id=0, has_side_effects=True, vmem_limit_bytes=53 << 20),
        name="sum_terms",
    )(terms)

    return pl.pallas_call(
        functools.partial(finish_kernel, users),
        out_shape=(
            jax.ShapeDtypeStruct((width, embed), f32),
            jax.ShapeDtypeStruct((table, embed), f32),
        ),
        in_specs=[smem, vmem, vmem],
        out_specs=(hbm, hbm),
        scratch_shapes=[
            pltpu.VMEM((width, embed), f32),
            pltpu.VMEM((table, embed), f32),
            dma((2,)),
        ],
        compiler_params=pltpu.CompilerParams(vmem_limit_bytes=8 << 20),
        name="finish",
    )(user_ids, part, user_terms)


def solution(mesh):
    return jax.shard_map(
        shards,
        mesh=mesh,
        in_specs=(
            P("shard", None),
            P(),
            P(),
            P(),
            P(),
            P(),
            P(("blk", "shard"), None),
            P(("blk", "shard")),
            P(("blk", "shard"), None),
            P(("blk", "shard"), None),
            P(("blk", "shard")),
        ),
        out_specs=(P("shard", None), P(("blk", "shard"), None)),
        check_vma=False,
    )
```
